32 devices in a mesh: dp: 8 (over y, x, core), seq: 4 (over z).
Axes of the slice: x: 2, y: 2, z: 4, core: 2. Of those that a mesh axis runs over, the one named last changes fastest.
Arguments:
- tokens: bfloat16 [16, 1024, 768], P('dp', 'seq'), may hold values from -6 to 6
- encoded: bfloat16 [16, 256, 768], P('dp', 'seq'), may hold values from -6 to 6
- cotangent: bfloat16 [16, 1024, 768], P('dp', 'seq'), may hold values from -6 to 6
- attn_in: bfloat16 [768, 2304], P('dp'), may hold values from -0.21875 to 0.21875
- attn_out: bfloat16 [768, 768], P('dp'), may hold values from -3.5 to 3.5
- cross_in: bfloat16 [768, 2304], P('dp'), may hold values from -0.21875 to 0.21875
- cross_out: bfloat16 [768, 768], P('dp'), may hold values from -3.5 to 3.5
- ffn_in: bfloat16 [768, 3072], P('dp'), may hold values from -0.21875 to 0.21875
- ffn_out: bfloat16 [3072, 768], P('dp'), may hold values from -0.109375 to 0.109375
- gains: bfloat16 [3, 768], P(None, 'dp'), may hold values from 0.5 to 1.5
- biases: bfloat16 [10, 768], P(None, 'dp'), may hold values from -1.5 to 1.5
- bias_ff: bfloat16 [3072], P('dp'), may hold values from -1.5 to 1.5
- block_ids: int32 [16, 1024], P('dp'), may hold values from 0 to 7, never falling along the last dimension, each value on 1 to 256 neighbouring positions
- enc_lengths: int32 [16], P('dp'), may hold values from 1 to 256, 3072 in all
Outputs:
- output: bfloat16 [16, 1024, 768], P('dp', 'seq')
- input_token_gradient: float32 [16, 1024, 768], P('dp', 'seq')
- encoded_grad: float32 [16, 256, 768], P('dp', 'seq')
- attn_in_grad: float32 [768, 2304], P('dp')
- attn_out_grad: float32 [768, 768], P('dp')
- cross_in_grad: float32 [768, 2304], P('dp')
- cross_out_grad: float32 [768, 768], P('dp')
- ffn_in_grad: float32 [768, 3072], P('dp')
- ffn_out_grad: float32 [3072, 768], P('dp')
- gains_grad: float32 [3, 768], P(None, 'dp')
- biases_grad: float32 [10, 768], P(None, 'dp')
- bias_ff_grad: float32 [3072], P('dp')
The draws below stay inside these ranges and needn't reach their ends.
Inputs may be any that keep to these rules, and one draw needn't show every extreme that they name: `block_ids`: along each sequence the ids never fall, every id from 0 to 7 occurs, and each id covers 1 to 256 tokens. `enc_lengths`: the lengths sum to 3072 and the largest is 256.
All inputs are finite; a program needn't handle non-finite values. No bound on the sum of `enc_lengths` on one device may be relied on, other than what follows from the above.
Results may differ from the reference program's by a relative error of at most 0.025.
Values may be sent and summed in bfloat16 or wider, within the bound.
No kernel may reach another device: no remote copies, remote signals or barrier semaphores. Data moves between devices by JAX's collectives and lax.ppermute only.
A program may use at most 256 MiB of HBM per device.

```python
import math
import jax
import jax.numpy as jnp
import numpy as np
from jax import lax

D = 768
H = 12
HD = 64
FF = 3072
LEN = 1024
ENC_LEN = 256
BLOCK = 256
SEQS = 16


def strengthened(drawn, stream_key, source, target, shards_of, factor):
    owner, partner = [(jnp.arange(drawn.shape[position]) // (drawn.shape[position] // shards_of)).reshape([-1 if axis == position else 1 for axis in range(drawn.ndim)]) for position in (source, target)]
    chosen = jax.random.permutation(stream_key, shards_of)[partner]
    strong = (owner == chosen) | (owner == (partner + shards_of // 2) % shards_of)
    return jnp.where(strong, factor * drawn, drawn)


def level_of(key, dims, shards, smallest, high):
    def one(position, shards_of):
        heights = jax.random.uniform(jax.random.fold_in(jax.random.fold_in(key, 6), position), (shards_of,), jnp.float32, smallest / len(shards), high / len(shards))
        return jnp.repeat(jnp.exp(heights), dims[position] // shards_of).reshape((-1,) + (1,) * (len(dims) - position - 1))

    level = one(*shards[0])
    for cut in shards[1:]:
        level = level * one(*cut)
    return level


def profile(number_of, total, bound, slope):
    weights = [(1 << 20) // math.isqrt(rank ** slope) + 1 for rank in range(2, number_of + 1)]
    rest, holding = total - bound - (number_of - 1), [1] * (number_of - 1)
    while rest > 0:
        candidates = [i for i in range(number_of - 1) if holding[i] < bound]
        mass, remaining = sum([weights[i] for i in candidates]), rest
        for i in candidates:
            extra = min(bound - holding[i], max(1, remaining * weights[i] // mass), rest)
            holding[i] = holding[i] + extra
            rest = rest - extra
    return np.array([bound] + holding)


def ragged(own_key, count, total, reach, skew):
    if count == 2:
        one = jax.random.randint(own_key, (), max(1, total - reach), min(reach, total - 1) + 1)
        return jnp.stack([one, total - one])
    sizes = jnp.asarray(profile(count, total, reach, skew), jnp.int32)
    couples = (count - 1) // 2
    donor, receiver = sizes[1:1 + 2 * couples:2], sizes[2:2 + 2 * couples:2]
    margin = jnp.minimum(donor - 1, reach - receiver)
    moved = jax.random.randint(jax.random.fold_in(own_key, 1), (couples,), 0, 1 << 20) % (margin + 1)
    sizes = sizes.at[1:1 + 2 * couples:2].set(donor - moved).at[2:2 + 2 * couples:2].set(receiver + moved)
    return sizes[jax.random.permutation(jax.random.fold_in(own_key, 2), count)]


def centred(rng, extent, scale, bound, pieces=(), kind=jnp.bfloat16):
    entries = scale * jax.random.normal(rng, extent, jnp.float32)
    if pieces:
        entries = entries * level_of(rng, extent, pieces, -0.22, 0.18)
    return jnp.clip(entries, -bound, bound).astype(kind)


def gaussian_with(key, shape, scale, bound, cuts, heavy, held_as=jnp.bfloat16):
    drawn = scale * jax.random.normal(key, shape, jnp.float32)
    if cuts:
        drawn = drawn * level_of(key, shape, cuts, -0.22, 0.18)
    return jnp.clip(strengthened(drawn, jax.random.fold_in(key, 3), *heavy), -bound, bound).astype(held_as)


def setup_inputs(seed: int = 0) -> dict:
    streams_of = jax.random.split(jax.random.key(seed), 15)
    return {
        "tokens": gaussian_with(streams_of[0], (SEQS, LEN, D), 1.0, 6.0, ((0, 8), (1, 4)), (0, 2, 8, 2.0)),
        "encoded": gaussian_with(streams_of[1], (SEQS, ENC_LEN, D), 1.0, 6.0, ((0, 8), (1, 4)), (0, 2, 8, 2.0)),
        "cotangent": centred(streams_of[2], (SEQS, LEN, D), 1.0, 6.0, ((0, 8), (1, 4))),
        "attn_in": centred(streams_of[3], (D, 3 * D), D ** -0.5, 0.21875, ((0, 8),)),
        "attn_out": centred(streams_of[4], (D, D), (max(D // 256, 1)) ** -0.5, 3.5, ((0, 8),)),
        "cross_in": centred(streams_of[5], (D, 3 * D), D ** -0.5, 0.21875, ((0, 8),)),
        "cross_out": centred(streams_of[6], (D, D), (max(D // 256, 1)) ** -0.5, 3.5, ((0, 8),)),
        "ffn_in": centred(streams_of[7], (D, FF), D ** -0.5, 0.21875, ((0, 8),)),
        "ffn_out": centred(streams_of[8], (FF, D), FF ** -0.5, 0.109375, ((0, 8),)),
        "gains": jnp.clip(1.0 + 0.1 * jax.random.normal(streams_of[9], (3, D), jnp.float32), 0.5, 1.5).astype(jnp.bfloat16),
        "biases": centred(streams_of[10], (10, D), 0.3, 1.5, ((1, 8),)),
        "bias_ff": centred(streams_of[11], (FF,), 0.3, 1.5, ((0, 8),)),
        "block_ids": jax.vmap(lambda own: jnp.searchsorted(jnp.cumsum(ragged(own, 2 * LEN // BLOCK, LEN, BLOCK, 0)), jnp.arange(LEN), side="right"))(jax.random.split(streams_of[12], SEQS)).reshape((SEQS, LEN)).astype(jnp.int32),
        "enc_lengths": ragged(streams_of[13], SEQS, SEQS * ENC_LEN * 3 // 4, ENC_LEN, 0).astype(jnp.int32),
    }


@jax.custom_vjp
def low(v):
    return lax.optimization_barrier(v.astype(jnp.bfloat16)).astype(jnp.float32)

@jax.custom_vjp
def low_back(v):
    return v

def low_keep(v):
    return (low(v), None)

def low_pass(kept, grad):
    return (grad,)

def back_keep(v):
    return (v, None)

def back_low(kept, grad):
    return (low(grad),)
low.defvjp(low_keep, low_pass)
low_back.defvjp(back_keep, back_low)
EPSILON = 1e-05
HIGHEST = lax.Precision.HIGHEST

def rounded_both(values):
    return low(low_back(values))

def matmul(left, right):
    return jnp.dot(left, right, precision=HIGHEST, preferred_element_type=jnp.float32)

def layer_norm(summed, gain, offset):
    centre = summed - lax.optimization_barrier(jnp.mean(summed, axis=-1, keepdims=True))
    spread = lax.optimization_barrier(jnp.mean(centre * centre, axis=-1, keepdims=True))
    return centre * lax.rsqrt(spread + EPSILON) * gain + offset

def split_heads(values):
    return values.reshape(values.shape[0], H, HD).transpose(1, 0, 2)

def attend(queries, keys_all, values_all, allowed):
    factor = float(HD) ** (-0.5)

    def one_head(head_items):
        single_query_head, single_key_head, value_head = head_items
        raw_scores = jnp.einsum('qe,ke->qk', single_query_head, single_key_head, precision=HIGHEST)
        scores = jnp.where(allowed, low_back(raw_scores) * factor, -1e+30)
        shifted = scores - lax.optimization_barrier(jnp.max(scores, axis=-1, keepdims=True))
        exponent = jnp.exp(shifted)
        softmax_weights = exponent / lax.optimization_barrier(jnp.sum(exponent, axis=-1, keepdims=True))
        return jnp.einsum('qk,ke->qe', low(softmax_weights), value_head, precision=HIGHEST)
    heads_out = lax.map(jax.checkpoint(one_head), (split_heads(queries), split_heads(keys_all), split_heads(values_all)))
    return heads_out.transpose(1, 0, 2).reshape(queries.shape[0], H * HD)

def forward(tokens, encoded, attn_in, attn_out, cross_in, cross_out, ffn_in, ffn_out, gains, biases, bias_ff, block_row, enc_valid):
    projected = matmul(tokens, attn_in)
    queries = rounded_both(projected[:, 0:D] + biases[0])
    keys_all = rounded_both(projected[:, D:2 * D])
    values_all = rounded_both(projected[:, 2 * D:3 * D] + biases[1])
    self_allowed = block_row[None, :] <= block_row[:, None]
    context = rounded_both(attend(queries, keys_all, values_all, self_allowed))
    attn_branch = low_back(matmul(context, attn_out) + biases[2])
    first = layer_norm(tokens + attn_branch, gains[0], biases[7])
    cross_queries = rounded_both(matmul(low(first), cross_in[:, 0:D]) + biases[3])
    enc_projected = matmul(encoded, cross_in[:, D:3 * D])
    cross_keys = rounded_both(enc_projected[:, 0:D])
    cross_values = rounded_both(enc_projected[:, D:2 * D] + biases[4])
    cross_allowed = (jnp.arange(ENC_LEN) < enc_valid)[None, :]
    cross_context = rounded_both(attend(cross_queries, cross_keys, cross_values, cross_allowed))
    cross_branch = low_back(matmul(cross_context, cross_out) + biases[5])
    second = layer_norm(first + cross_branch, gains[1], biases[8])
    activation = low_back(matmul(low(second), ffn_in) + bias_ff)
    hidden = low(jax.nn.gelu(activation, approximate=False))
    ffn_branch = low_back(matmul(hidden, ffn_out) + biases[6])
    return layer_norm(second + ffn_branch, gains[2], biases[9])

def reference(tokens, encoded, cotangent, attn_in, attn_out, cross_in, cross_out, ffn_in, ffn_out, gains, biases, bias_ff, block_ids, enc_lengths):
    params = tuple((weight.astype(jnp.float32) for weight in (attn_in, attn_out, cross_in, cross_out, ffn_in, ffn_out, gains, biases, bias_ff)))
    starting = tuple((jnp.zeros(weight.shape, jnp.float32) for weight in params))

    def sequence_step(totals, sequence_items):
        seq_tokens, seq_encoded, seq_cotangent, block_row, enc_valid = sequence_items

        def layer_forward(tokens_float, encoded_float, *weights):
            return forward(tokens_float, encoded_float, *weights, block_row, enc_valid)
        result, pull_back = jax.vjp(layer_forward, seq_tokens.astype(jnp.float32), seq_encoded.astype(jnp.float32), *params)
        gradients = pull_back(seq_cotangent.astype(jnp.float32))
        totals = tuple((running + grad_piece for running, grad_piece in zip(totals, gradients[2:])))
        return (totals, (result.astype(jnp.bfloat16), gradients[0], gradients[1]))
    totals, stacked = lax.scan(sequence_step, starting, (tokens, encoded, cotangent, block_ids, enc_lengths))
    return (stacked[0], stacked[1], stacked[2], totals[0], totals[1], totals[2], totals[3], totals[4], totals[5], totals[6], totals[7], totals[8])
```

```python
import jax
import jax.numpy as jnp
from jax import lax
from jax.experimental import pallas as pl
from jax.experimental.pallas import tpu as pltpu
from jax.sharding import PartitionSpec as P

HD = 64
PAIR = 2 * HD
EPSILON = 1e-05
MASKED = -1e30
LOW = jnp.bfloat16
WIDE = jnp.float32


def product(left, right):
    return jnp.dot(left, right, preferred_element_type=WIDE)


def left_transposed(left, right):
    return lax.dot_general(left, right, (((0,), (0,)), ((), ())), preferred_element_type=WIDE)


def right_transposed(left, right):
    return lax.dot_general(left, right, (((1,), (1,)), ((), ())), preferred_element_type=WIDE)


def column_total(values):
    return jnp.sum(values.astype(WIDE), axis=0)


def layer_norm(summed, gain, offset):
    centre = summed - jnp.mean(summed, axis=-1, keepdims=True)
    spread = jnp.mean(centre * centre, axis=-1, keepdims=True)
    return centre * lax.rsqrt(spread + EPSILON) * gain + offset


def norm_backward(summed, gain, upstream):
    centre = summed - jnp.mean(summed, axis=-1, keepdims=True)
    spread = jnp.mean(centre * centre, axis=-1, keepdims=True)
    inverse = lax.rsqrt(spread + EPSILON)
    unit = centre * inverse
    scaled = upstream * gain
    mean_scaled = jnp.mean(scaled, axis=-1, keepdims=True)
    mean_both = jnp.mean(scaled * unit, axis=-1, keepdims=True)
    d_summed = (scaled - mean_scaled - unit * mean_both) * inverse
    return d_summed, jnp.sum(upstream * unit, axis=0), jnp.sum(upstream, axis=0)


def stacked_heads(values):
    lane = lax.broadcasted_iota(jnp.int32, values.shape, 1)
    none = jnp.zeros_like(values)
    return jnp.concatenate(
        [jnp.where(lane < HD, values, none), jnp.where(lane >= HD, values, none)], axis=0
    )


def merged_heads(stacked):
    half = stacked.shape[0] // 2
    lane = lax.broadcasted_iota(jnp.int32, (half, PAIR), 1)
    return jnp.where(lane < HD, stacked[:half], stacked[half:])


def forward_kernel(q_ref, kv_ref, qid_ref, kid_ref, o_ref, total_ref):
    queries = stacked_heads(q_ref[0]) * jnp.asarray(HD**-0.5, LOW)
    scores = right_transposed(queries, kv_ref[0, :, :PAIR])
    qid = qid_ref[0]
    allowed = kid_ref[0] <= jnp.concatenate([qid, qid], axis=0)
    scores = jnp.where(allowed, scores, MASKED)
    highest = jnp.max(scores, axis=-1, keepdims=True)
    exponent = jnp.exp(scores - highest)
    denominator = jnp.sum(exponent, axis=-1, keepdims=True)
    context = product(exponent.astype(LOW), kv_ref[0, :, PAIR:]) / denominator
    o_ref[0] = merged_heads(context).astype(LOW)
    totals = highest + jnp.log(denominator)
    total_ref[0, 0] = jnp.transpose(jnp.broadcast_to(totals, (totals.shape[0], 128)))[:8]


def backward_kernel(q_ref, kv_ref, qid_ref, kid_ref, o_ref, do_ref, total_ref, dq_ref, dkv_ref):
    queries = stacked_heads(q_ref[0]) * jnp.asarray(HD**-0.5, LOW)
    upstream = stacked_heads(do_ref[0])
    both = do_ref[0].astype(WIDE) * o_ref[0].astype(WIDE)
    row = lax.broadcasted_iota(jnp.int32, (8, PAIR), 0)
    lane = lax.broadcasted_iota(jnp.int32, (8, PAIR), 1)
    pick = jnp.where(lane // HD == row, 1.0, 0.0).astype(WIDE)
    inner = lax.dot_general(
        pick,
        both,
        (((1,), (1,)), ((), ())),
        precision=lax.Precision.HIGHEST,
        preferred_element_type=WIDE,
    )
    inner = jnp.concatenate([inner[0:1], inner[1:2]], axis=1)
    keys = kv_ref[0, :, :PAIR]
    qid = qid_ref[0]
    allowed = kid_ref[0] <= jnp.concatenate([qid, qid], axis=1)
    scores = jnp.where(allowed, right_transposed(keys, queries), MASKED)
    weights = jnp.exp(scores - total_ref[0, 0, 0:1])
    dkv_ref[0, :, PAIR:] = product(weights.astype(LOW), upstream).astype(LOW)
    weight_grads = right_transposed(kv_ref[0, :, PAIR:], upstream)
    score_grads = (weights * (weight_grads - inner)).astype(LOW)
    dkv_ref[0, :, :PAIR] = product(score_grads, queries).astype(LOW)
    dq = left_transposed(score_grads, keys) * (HD**-0.5)
    dq_ref[0] = merged_heads(dq).astype(LOW)


def attend_forward(queries, keys_values, ids):
    batch, rows, width = queries.shape
    keys = keys_values.shape[1]
    pairs = width // PAIR
    one = pl.BlockSpec((1, rows, PAIR), lambda b, p: (b, 0, p))
    work = batch * pairs * rows * keys
    return pl.pallas_call(
        forward_kernel,
        grid=(batch, pairs),
        in_specs=[
            one,
            pl.BlockSpec((1, keys, 2 * PAIR), lambda b, p: (b, 0, p)),
            pl.BlockSpec((1, rows, 1), lambda b, p: (b, 0, 0)),
            pl.BlockSpec((1, 1, keys), lambda b, p: (b, 0, 0)),
        ],
        out_specs=[one, pl.BlockSpec((1, 1, 8, 2 * rows), lambda b, p: (b, p, 0, 0))],
        out_shape=[
            jax.ShapeDtypeStruct((batch, rows, width), LOW),
            jax.ShapeDtypeStruct((batch, pairs, 8, 2 * rows), WIDE),
        ],
        cost_estimate=pl.CostEstimate(
            flops=4000 * work, transcendentals=2 * work, bytes_accessed=8 * batch * keys * width
        ),
        name="attend_forward",
    )(queries, keys_values, ids[3], ids[0])


def attend_backward(queries, keys_values, ids, context, upstream, totals, start, count):
    _, rows, width = queries.shape
    keys = keys_values.shape[1]
    pairs = width // PAIR
    one = pl.BlockSpec((1, rows, PAIR), lambda b, p: (start + b, 0, p))
    work = count * pairs * rows * keys
    return pl.pallas_call(
        backward_kernel,
        grid=(count, pairs),
        in_specs=[
            one,
            pl.BlockSpec((1, keys, 2 * PAIR), lambda b, p: (start + b, 0, p)),
            pl.BlockSpec((1, 1, rows), lambda b, p: (start + b, 0, 0)),
            pl.BlockSpec((1, keys, 1), lambda b, p: (start + b, 0, 0)),
            one,
            one,
            pl.BlockSpec((1, 1, 8, 2 * rows), lambda b, p: (start + b, p, 0, 0)),
        ],
        out_specs=[
            pl.BlockSpec((1, rows, PAIR), lambda b, p: (b, 0, p)),
            pl.BlockSpec((1, keys, 2 * PAIR), lambda b, p: (b, 0, p)),
        ],
        out_shape=[
            jax.ShapeDtypeStruct((count, rows, width), LOW),
            jax.ShapeDtypeStruct((count, keys, 2 * width), LOW),
        ],
        cost_estimate=pl.CostEstimate(
            flops=4000 * work, transcendentals=2 * work, bytes_accessed=8 * count * keys * width
        ),
        name="attend_backward",
    )(queries, keys_values, ids[2], ids[1], context, upstream, totals)


CHUNK = 512


def normalised(summed):
    centre = summed - jnp.mean(summed, axis=-1, keepdims=True)
    inverse = lax.rsqrt(jnp.mean(centre * centre, axis=-1, keepdims=True) + EPSILON)
    return centre * inverse, inverse


def normalised_backward(unit, inverse, scaled):
    mean_scaled = jnp.mean(scaled, axis=-1, keepdims=True)
    mean_both = jnp.mean(scaled * unit, axis=-1, keepdims=True)
    return (scaled - mean_scaled - unit * mean_both) * inverse


def gelu_pair(values):
    size = jnp.abs(values) * (0.5**0.5)
    bell = jnp.exp(-0.5 * values * values)
    t = 1.0 / (1.0 + 0.3275911 * size)
    series = t * (
        0.127414796
        + t * (-0.142248368 + t * (0.7107068705 + t * (-0.7265760135 + t * 0.5307027145)))
    )
    tail = series * bell
    below = jnp.where(values >= 0, 1.0 - tail, tail)
    return values * below, below + values * bell * 0.3989422804014327


def total_row(values):
    return jnp.sum(values, axis=0, keepdims=True)


def ffn_kernel(
    first_ref,
    cross_ref,
    cot_ref,
    vector_ref,
    hidden_bias_ref,
    early_ref,
    in_ref,
    out_ref,
    final_ref,
    d_sum_ref,
    d_ctx_ref,
    g_cross_ref,
    sums_ref,
    hidden_sums_ref,
    g_in_ref,
    g_out_ref,
    w_cross,
    w_in,
    w_out,
    hidden,
    slope,
    total,
    low,
    d_low,
    g_in,
    g_out,
    load_sem,
    in_sem,
    out_sem,
):
    rows, width = first_ref.shape
    count = w_in.shape[1] // CHUNK
    cross_at = early_ref.shape[1] - width
    loads = [
        pltpu.make_async_copy(early_ref.at[:, cross_at:], w_cross, load_sem.at[0]),
        pltpu.make_async_copy(in_ref, w_in, load_sem.at[1]),
        pltpu.make_async_copy(out_ref, w_out, load_sem.at[2]),
    ]
    for load in loads:
        load.start()
    loads[0].wait()
    second_sum = first_ref[...] + product(cross_ref[...], w_cross[...]) + vector_ref[0:1]
    unit, inverse = normalised(second_sum)
    second = unit * vector_ref[1:2] + vector_ref[2:3]
    low[...] = second.astype(LOW)
    total[...] = second + vector_ref[3:4]
    d_sum_ref[...] = unit
    loads[1].wait()
    loads[2].wait()

    def forward(step, carry):
        at = pl.ds(pl.multiple_of(step * CHUNK, CHUNK), CHUNK)
        activation = product(low[...], w_in[:, at]) + hidden_bias_ref[:, at]
        value, slope_value = gelu_pair(activation)
        value = value.astype(LOW)
        hidden[:, at] = value
        slope[:, at] = slope_value
        total[...] += product(value, w_out[at, :])
        return carry

    lax.fori_loop(0, count, forward, 0)
    third, third_inverse = normalised(total[...])
    final_ref[...] = (third * vector_ref[4:5] + vector_ref[5:6]).astype(LOW)
    upstream = cot_ref[...].astype(WIDE)
    sums_ref[0:1] = total_row(upstream * third)
    sums_ref[1:2] = total_row(upstream)
    d_third = normalised_backward(third, third_inverse, upstream * vector_ref[4:5])
    d_low[...] = d_third.astype(LOW)
    sums_ref[2:3] = total_row(d_low[...].astype(WIDE))
    total[...] = d_third

    def copies(step):
        at = pl.ds(pl.multiple_of(step * CHUNK, CHUNK), CHUNK)
        return (
            pltpu.make_async_copy(g_in.at[:, at], g_in_ref.at[:, at], in_sem.at[step]),
            pltpu.make_async_copy(g_out.at[at, :], g_out_ref.at[at, :], out_sem.at[step]),
        )

    def backward(step, carry):
        at = pl.ds(pl.multiple_of(step * CHUNK, CHUNK), CHUNK)
        g_out[at, :] = left_transposed(hidden[:, at], d_low[...]).astype(LOW)
        d_hidden = right_transposed(d_low[...], w_out[at, :])
        d_activation = (d_hidden * slope[:, at]).astype(LOW)
        hidden_sums_ref[:, at] = total_row(d_activation.astype(WIDE))
        g_in[:, at] = left_transposed(low[...], d_activation).astype(LOW)
        total[...] += right_transposed(d_activation, w_in[:, at])
        for copy in copies(step):
            copy.start()
        return carry

    lax.fori_loop(0, count, backward, 0)
    d_second = total[...]
    unit = d_sum_ref[...]
    sums_ref[3:4] = total_row(d_second * unit)
    sums_ref[4:5] = total_row(d_second)
    d_second_sum = normalised_backward(unit, inverse, d_second * vector_ref[1:2])
    d_sum_ref[...] = d_second_sum
    d_cross = d_second_sum.astype(LOW)
    sums_ref[5:6] = total_row(d_cross.astype(WIDE))
    d_ctx = right_transposed(d_cross, w_cross[...]).astype(LOW)
    d_ctx_ref[...] = d_ctx
    sums_ref[6:7] = total_row(d_ctx.astype(WIDE))
    sums_ref[7:8] = jnp.zeros_like(sums_ref[7:8])
    g_cross_ref[...] = left_transposed(cross_ref[...], d_cross).astype(LOW)

    def drain(step, carry):
        for copy in copies(step):
            copy.wait()
        return carry

    lax.fori_loop(0, count, drain, 0)


def ffn_stage(first, cross, cotangent, vectors, hidden_bias, early, ffn_in, ffn_out):
    rows, width = first.shape
    hidden_width = ffn_in.shape[1]
    count = hidden_width // CHUNK
    inside = pl.BlockSpec(memory_space=pltpu.VMEM)
    outside = pl.BlockSpec(memory_space=pl.ANY)
    return pl.pallas_call(
        ffn_kernel,
        in_specs=[inside] * 5 + [outside] * 3,
        out_specs=[inside] * 6 + [outside] * 2,
        out_shape=[
            jax.ShapeDtypeStruct((rows, width), LOW),
            jax.ShapeDtypeStruct((rows, width), WIDE),
            jax.ShapeDtypeStruct((rows, width), LOW),
            jax.ShapeDtypeStruct((width, width), LOW),
            jax.ShapeDtypeStruct((8, width), WIDE),
            jax.ShapeDtypeStruct((1, hidden_width), WIDE),
            jax.ShapeDtypeStruct((width, hidden_width), LOW),
            jax.ShapeDtypeStruct((hidden_width, width), LOW),
        ],
        scratch_shapes=[
            pltpu.VMEM((width, width), LOW),
            pltpu.VMEM((width, hidden_width), LOW),
            pltpu.VMEM((hidden_width, width), LOW),
            pltpu.VMEM((rows, hidden_width), LOW),
            pltpu.VMEM((rows, hidden_width), WIDE),
            pltpu.VMEM((rows, width), WIDE),
            pltpu.VMEM((rows, width), LOW),
            pltpu.VMEM((rows, width), LOW),
            pltpu.VMEM((width, hidden_width), LOW),
            pltpu.VMEM((hidden_width, width), LOW),
            pltpu.SemaphoreType.DMA((3,)),
            pltpu.SemaphoreType.DMA((count,)),
            pltpu.SemaphoreType.DMA((count,)),
        ],
        compiler_params=pltpu.CompilerParams(vmem_limit_bytes=58 << 20),
        cost_estimate=pl.CostEstimate(
            flops=16 * rows * width * hidden_width,
            transcendentals=rows * hidden_width,
            bytes_accessed=12 * width * hidden_width,
        ),
        name="ffn_stage",
    )(first, cross, cotangent, vectors, hidden_bias, early, ffn_in, ffn_out)


def gathered_back(own, groups):
    place = lax.axis_index("seq")
    behind = lax.ppermute(own, "seq", [(source, source + 1) for source in range(groups - 1)])
    ahead = lax.ppermute(own, "seq", [(source, source - 1) for source in range(1, groups)])
    if groups == 4:
        last = lax.ppermute(own, "seq", [(0, 3)])
        going = jnp.where(place == 2, behind, own)
        slots = [own, behind, lax.ppermute(going, "seq", [(0, 2), (2, 3)])]
    else:
        slots = [own, behind]
        for step in range(2, groups):
            pairs = [(source, source + 1) for source in range(step - 1, groups - 1)]
            slots.append(lax.ppermute(slots[-1], "seq", pairs))
        last = slots.pop()
    return slots + [jnp.where(place == groups - 1, last, ahead)]


def scatter_back(slots, groups):
    parts = []
    for step in range(groups - 1, 0, -1):
        pairs = [(source, source - step) for source in range(step, groups)]
        parts.append(lax.ppermute(slots[step], "seq", pairs))
    pairs = [(source, source + 1) for source in range(groups - 1)]
    parts.append(lax.ppermute(slots[groups - 1], "seq", pairs))
    return parts


def tied(value, *others):
    return lax.optimization_barrier((value,) + others)[0]


def by_bit(bit, own, other, axis=0):
    own, other = jnp.expand_dims(own, axis), jnp.expand_dims(other, axis)
    return jnp.where(
        bit == 0,
        jnp.concatenate([own, other], axis=axis),
        jnp.concatenate([other, own], axis=axis),
    )


def crossed(value, axis_name, masks):
    count = lax.axis_size(axis_name)
    pairs = [(source, source ^ masks[source % len(masks)]) for source in range(count)]
    return lax.ppermute(value, axis_name, pairs)


CORE = (1,)
FIRST = (2, 4)
SECOND = (4, 2)


def chip_masks(core):
    first = jnp.where(core == 0, 1, 2)
    return first, 3 - first


def gather_rows(shard):
    return lax.all_gather(shard, "dp", axis=0, tiled=True)


def picked(values, position, axis=0):
    return lax.dynamic_index_in_dim(values, position, axis, keepdims=False)


def plus(left, right):
    return (left.astype(WIDE) + right.astype(WIDE)).astype(LOW)


class Chain:
    def __init__(self, steps):
        self.steps = steps
        self.pending = next(steps)
        self.result = None

    def step(self):
        if self.result is None:
            try:
                self.pending = self.steps.send(self.pending)
            except StopIteration as stop:
                self.result = stop.value


def pumped(values, *chains):
    live = [chain for chain in chains if chain.result is None]
    values, arrived = lax.optimization_barrier((values, [chain.pending for chain in live]))
    for chain, brought in zip(live, arrived):
        chain.pending = brought
        chain.step()
    return values


def finished(*chains):
    while any(chain.result is None for chain in chains):
        for chain in chains:
            chain.step()
    return [chain.result for chain in chains]


def places_steps(sums):
    place = lax.axis_index("seq")
    low_bit, high_bit = place % 2, place // 2
    sums = sums.reshape((2, 2) + sums.shape[1:])
    sums = plus(picked(sums, low_bit, 1), (yield crossed(picked(sums, 1 - low_bit, 1), "seq", (1,))))
    sums = plus(picked(sums, high_bit), (yield crossed(picked(sums, 1 - high_bit), "seq", (2,))))
    sums = by_bit(high_bit, sums, (yield crossed(sums, "seq", (2,))))
    return by_bit(low_bit, sums, (yield crossed(sums, "seq", (1,))), 1)


def offloaded_steps(gradient):
    share = yield lax.psum_scatter(gradient, "dp", scatter_dimension=0, tiled=True)
    if lax.axis_size("dp") != 8 or lax.axis_size("seq") != 4:
        return (yield lax.psum(share, "seq")).astype(WIDE)
    rows, columns = share.shape
    sums = yield from places_steps(share.reshape(4, rows // 4, columns))
    return sums.reshape(rows, columns).astype(WIDE)


def exchange_steps(gradient):
    if lax.axis_size("dp") != 8 or lax.axis_size("seq") != 4:
        return (yield from offloaded_steps(gradient))
    index = lax.axis_index("dp")
    core, chip = index % 2, index // 2
    first, second = chip_masks(core)
    rows, columns = gradient.shape
    half = rows // 16
    view = gradient.reshape(4, 2, 2, half, columns)
    sums = plus(picked(view, core, 2), (yield crossed(picked(view, 1 - core, 2), "dp", CORE)))
    going = jnp.stack([picked(sums, chip ^ first), picked(sums, chip ^ 3)])
    kept = jnp.stack([picked(sums, chip), picked(sums, chip ^ second)])
    sums = plus(kept, (yield crossed(going, "dp", FIRST)))
    sums = plus(sums[0], (yield crossed(sums[1], "dp", SECOND)))
    sums = yield from places_steps(sums.reshape(4, half // 2, columns))
    sums = sums.reshape(2, half, columns)
    own = by_bit(core, picked(sums, core), (yield crossed(picked(sums, 1 - core), "dp", CORE)))
    return own.reshape(2 * half, columns).astype(WIDE)


def gather_small(values):
    if lax.axis_size("dp") != 8:
        return lax.all_gather(values, "dp", axis=0)
    index = lax.axis_index("dp")
    out = by_bit(index % 2, values, crossed(values, "dp", CORE))
    out = by_bit(index // 2 % 2, out, crossed(out, "dp", (2,)))
    out = by_bit(index // 4, out, crossed(out, "dp", (4,)))
    return out.reshape((8,) + values.shape)


def small_steps(values):
    if lax.axis_size("dp") != 8 or lax.axis_size("seq") != 4:
        return (yield lax.psum(values, ("dp", "seq")))
    for axis_name, mask in (("dp", 1), ("dp", 2), ("dp", 4), ("seq", 1), ("seq", 2)):
        values = values + (yield crossed(values, axis_name, (mask,)))
    return values


def gather_steps(values):
    if lax.axis_size("seq") != 4:
        return (yield lax.all_gather(values, "seq", axis=0))
    place = lax.axis_index("seq")
    out = by_bit(place % 2, values, (yield crossed(values, "seq", (1,))))
    out = by_bit(place // 2, out, (yield crossed(out, "seq", (2,))))
    return out.reshape((4,) + values.shape)


def chunk_steps(values):
    if lax.axis_size("seq") != 4:
        return (yield lax.psum_scatter(values, "seq", scatter_dimension=0, tiled=False)).astype(WIDE)
    place = lax.axis_index("seq")
    low_bit, high_bit = place % 2, place // 2
    values = values.reshape((2, 2) + values.shape[1:])
    going = picked(values, 1 - low_bit, 1)
    values = plus(picked(values, low_bit, 1), (yield crossed(going, "seq", (1,))))
    going = picked(values, 1 - high_bit)
    return picked(values, high_bit).astype(WIDE) + (yield crossed(going, "seq", (2,))).astype(WIDE)


def interleaved(keys_values):
    rows, columns = keys_values.shape
    view = keys_values.reshape(rows, 2, columns // (2 * PAIR), PAIR)
    return view.transpose(0, 2, 1, 3).reshape(rows, columns)


def deinterleaved(keys_values):
    rows, columns = keys_values.shape
    view = keys_values.reshape(rows, columns // (2 * PAIR), 2, PAIR)
    return view.transpose(0, 2, 1, 3).reshape(rows, columns)


def local(
    tokens,
    encoded,
    cotangent,
    attn_in,
    attn_out,
    cross_in,
    cross_out,
    ffn_in,
    ffn_out,
    gains,
    biases,
    bias_ff,
    block_ids,
    enc_lengths,
):
    groups = lax.axis_size("seq")
    shards = lax.axis_size("dp")
    place = lax.axis_index("seq")
    owner = lax.axis_index("dp")
    batch, local_len, width = tokens.shape
    enc_local = encoded.shape[1]
    rows = batch * local_len
    length = local_len * groups
    enc_length = enc_local * groups
    hidden_width = ffn_in.shape[1]

    attn_q, attn_kv = attn_in[:, :width], interleaved(attn_in[:, width:])
    cross_q, cross_kv = cross_in[:, :width], interleaved(cross_in[:, width:])
    early = gather_rows(
        jnp.concatenate([attn_q, attn_kv, attn_out, cross_q, cross_kv, cross_out], axis=1)
    )
    slots = gathered_back(tokens, groups)
    small = jnp.concatenate([gains, biases, bias_ff.reshape(-1, gains.shape[1])], axis=0)
    small = gather_small(small)
    small = small.astype(WIDE)
    gain_rows = gains.shape[0]
    bias_rows = biases.shape[0]
    vectors = small[:, : gain_rows + bias_rows].transpose(1, 0, 2).reshape(-1, width)
    gain_all = vectors[:gain_rows]
    bias_all = vectors[gain_rows:]
    bias_hidden = small[:, gain_rows + bias_rows :].reshape(hidden_width)
    blank = jnp.zeros((width,), WIDE)
    value_bias = interleaved(jnp.concatenate([blank, bias_all[1]])[None])
    cross_value_bias = interleaved(jnp.concatenate([blank, bias_all[4]])[None])

    chunks = block_ids.reshape(batch, groups, local_len)
    order = (place - jnp.arange(groups)) % groups
    kid = jnp.take(chunks, order, axis=1).reshape(batch, length)
    qid = kid[:, :local_len]
    enc_kid = jnp.broadcast_to(jnp.arange(enc_length, dtype=jnp.int32)[None], (batch, enc_length))
    enc_qid = jnp.broadcast_to(enc_lengths[:, None] - 1, (batch, local_len))
    ids = (kid[:, None, :], kid[:, :, None], qid[:, None, :], qid[:, :, None])
    enc_ids = (enc_kid[:, None, :], enc_kid[:, :, None], enc_qid[:, None, :], enc_qid[:, :, None])

    vectors = (gain_all, bias_all, bias_hidden, value_bias, cross_value_bias)
    early, slots, vectors, ids, enc_ids = lax.optimization_barrier(
        (early, slots, vectors, ids, enc_ids)
    )
    gain_all, bias_all, bias_hidden, value_bias, cross_value_bias = vectors
    attn_q, attn_kv = early[:, :width], early[:, width : 3 * width]
    attn_out, cross_q = early[:, 3 * width : 4 * width], early[:, 4 * width : 5 * width]
    cross_kv = early[:, 5 * width : 7 * width]
    ffn_in = gather_rows(ffn_in)
    ffn_out = gather_rows(ffn_out)
    enc_gather = Chain(gather_steps(tied(encoded, slots[-1])))

    token_all = jnp.concatenate(slots, axis=1).reshape(batch * length, width)
    token_flat = tokens.reshape(rows, width)
    queries = (product(token_flat, attn_q) + bias_all[0]).astype(LOW)
    queries = queries.reshape(batch, local_len, width)
    keys_values = (product(token_all, attn_kv) + value_bias).astype(LOW)
    keys_values = keys_values.reshape(batch, length, 2 * width)

    queries, keys_values = pumped((queries, keys_values), enc_gather)
    context, totals = attend_forward(queries, keys_values, ids)
    context = pumped(context, enc_gather)
    encoded = enc_gather.result
    enc_all = encoded.transpose(1, 0, 2, 3).reshape(batch * enc_length, width)
    enc_kv = (product(enc_all, cross_kv) + cross_value_bias).astype(LOW)
    enc_kv = enc_kv.reshape(batch, enc_length, 2 * width)
    context_flat = context.reshape(rows, width)
    first_sum = token_flat.astype(WIDE) + product(context_flat, attn_out) + bias_all[2]
    first = layer_norm(first_sum, gain_all[0], bias_all[7])
    first_low = first.astype(LOW)
    cross_queries = (product(first_low, cross_q) + bias_all[3]).astype(LOW)
    cross_queries = cross_queries.reshape(batch, local_len, width)
    cross_context, cross_totals = attend_forward(cross_queries, enc_kv, enc_ids)
    cross_flat = cross_context.reshape(rows, width)
    stage_vectors = jnp.stack(
        [bias_all[5], gain_all[1], bias_all[8], bias_all[6], gain_all[2], bias_all[9]]
    )
    final, d_second_sum, d_cross_ctx, grad_cross_out, sums, d_bias_hidden, grad_in, grad_out = (
        ffn_stage(
            first,
            cross_flat,
            cotangent.reshape(rows, width),
            stage_vectors,
            bias_hidden[None],
            early,
            ffn_in,
            ffn_out,
        )
    )
    out_chain = Chain(offloaded_steps(grad_out))
    in_chain = Chain(offloaded_steps(grad_in))
    d_cross_ctx = d_cross_ctx.reshape(cross_context.shape)
    d_cross_q, d_enc = attend_backward(
        cross_queries, enc_kv, enc_ids, cross_context, d_cross_ctx, cross_totals, 0, batch
    )
    d_cross_q = d_cross_q.reshape(rows, width)
    d_enc = d_enc.reshape(-1, 2 * width)
    grad_cross_q = left_transposed(first_low, d_cross_q)
    grad_cross_kv = left_transposed(enc_all, d_enc)
    d_encoded = right_transposed(d_enc, cross_kv).reshape(batch, groups, enc_local, width)
    enc_chain = Chain(chunk_steps(d_encoded.astype(LOW).transpose(1, 0, 2, 3)))
    d_first = d_second_sum + right_transposed(d_cross_q, cross_q)
    d_first_sum, d_gain_one, d_offset_one = norm_backward(first_sum, gain_all[0], d_first)
    d_attn = d_first_sum.astype(LOW)
    middle = [left_transposed(context_flat, d_attn), grad_cross_q, grad_cross_kv, grad_cross_out]
    middle = jnp.concatenate([part.astype(LOW) for part in middle], axis=1)
    mid_chain = Chain(exchange_steps(middle))
    d_context = right_transposed(d_attn, attn_out).astype(LOW).reshape(context.shape)

    d_context = pumped(d_context, out_chain)
    d_queries, d_keys_values, d_parts = [], [], []
    for start in range(batch):
        d_q, d_kv = attend_backward(
            queries, keys_values, ids, context, d_context, totals, start, 1
        )
        d_q, d_kv, d_context = pumped((d_q, d_kv, d_context), mid_chain, out_chain, enc_chain)
        d_part = right_transposed(d_kv[0], attn_kv).astype(LOW)
        d_part = d_part.reshape(groups, local_len, width)
        d_parts.append([d_part[0]] + scatter_back(list(d_part), groups))
        d_queries.append(d_q)
        d_keys_values.append(d_kv)
    d_query = jnp.concatenate(d_queries, axis=0).reshape(rows, width)
    d_kv = jnp.concatenate(d_keys_values, axis=0).reshape(batch * length, 2 * width)
    d_query, d_kv = pumped((d_query, d_kv), mid_chain, out_chain)
    grad_attn = jnp.concatenate(
        [
            left_transposed(token_flat, d_query).astype(LOW),
            left_transposed(token_all, d_kv).astype(LOW),
        ],
        axis=1,
    )
    grad_attn = pumped(grad_attn, mid_chain, in_chain, enc_chain)
    attn_chain = Chain(exchange_steps(grad_attn))
    vector_grads = jnp.stack(
        [
            d_gain_one,
            sums[3],
            sums[0],
            column_total(d_query),
            column_total(d_context.reshape(rows, width)),
            column_total(d_attn),
            column_total(d_cross_q),
            sums[6],
            sums[5],
            sums[2],
            d_offset_one,
            sums[4],
            sums[1],
        ]
    )
    vector_grads = jnp.concatenate([vector_grads, d_bias_hidden.reshape(-1, width)], axis=0)
    small_chain = Chain(small_steps(vector_grads))
    d_tokens = d_first_sum + right_transposed(d_query, attn_q)
    d_tokens = d_tokens.reshape(tokens.shape)
    grad_attn, middle, grad_ffn_out, grad_ffn_in, d_encoded, vector_grads = finished(
        attn_chain, mid_chain, out_chain, in_chain, enc_chain, small_chain
    )
    d_tokens = jnp.stack(
        [
            sum([part.astype(WIDE) for part in parts], d_tokens[number])
            for number, parts in enumerate(d_parts)
        ]
    )
    grad_attn_in = jnp.concatenate(
        [grad_attn[:, :width], deinterleaved(grad_attn[:, width:])], axis=1
    )
    grad_cross_in = jnp.concatenate(
        [middle[:, width : 2 * width], deinterleaved(middle[:, 2 * width : 4 * width])], axis=1
    )
    flat_hidden = vector_grads[gain_rows + bias_rows :].reshape(-1)
    part = width // shards
    mine = lax.dynamic_slice_in_dim(vector_grads, owner * part, part, axis=1)
    hidden_part = hidden_width // shards
    grad_bias_ff = lax.dynamic_slice_in_dim(flat_hidden, owner * hidden_part, hidden_part)
    return (
        final.reshape(batch, local_len, width),
        d_tokens,
        d_encoded,
        grad_attn_in,
        middle[:, :width],
        grad_cross_in,
        middle[:, 4 * width :],
        grad_ffn_in,
        grad_ffn_out,
        mine[:gain_rows],
        mine[gain_rows : gain_rows + bias_rows],
        grad_bias_ff,
    )


def solution(mesh):
    split = P("dp", "seq", None)
    rows = P("dp", None)
    columns = P(None, "dp")
    vector = P("dp")
    in_specs = (split,) * 3 + (rows,) * 6 + (columns, columns, vector, rows, vector)
    out_specs = (split,) * 3 + (rows,) * 6 + (columns, columns, vector)
    return jax.shard_map(local, mesh=mesh, in_specs=in_specs, out_specs=out_specs, check_vma=False)
```

```python
import jax
import jax.numpy as jnp
from jax import lax
from jax.experimental import pallas as pl
from jax.experimental.pallas import tpu as pltpu
from jax.sharding import PartitionSpec as P

HD = 64
PAIR = 2 * HD
EPSILON = 1e-05
MASKED = -1e30
LOW = jnp.bfloat16
WIDE = jnp.float32


def product(left, right):
    return jnp.dot(left, right, preferred_element_type=WIDE)


def left_transposed(left, right):
    return lax.dot_general(left, right, (((0,), (0,)), ((), ())), preferred_element_type=WIDE)


def right_transposed(left, right):
    return lax.dot_general(left, right, (((1,), (1,)), ((), ())), preferred_element_type=WIDE)


def column_total(values):
    return jnp.sum(values.astype(WIDE), axis=0)


def layer_norm(summed, gain, offset):
    centre = summed - jnp.mean(summed, axis=-1, keepdims=True)
    spread = jnp.mean(centre * centre, axis=-1, keepdims=True)
    return centre * lax.rsqrt(spread + EPSILON) * gain + offset


def norm_backward(summed, gain, upstream):
    centre = summed - jnp.mean(summed, axis=-1, keepdims=True)
    spread = jnp.mean(centre * centre, axis=-1, keepdims=True)
    inverse = lax.rsqrt(spread + EPSILON)
    unit = centre * inverse
    scaled = upstream * gain
    mean_scaled = jnp.mean(scaled, axis=-1, keepdims=True)
    mean_both = jnp.mean(scaled * unit, axis=-1, keepdims=True)
    d_summed = (scaled - mean_scaled - unit * mean_both) * inverse
    return d_summed, jnp.sum(upstream * unit, axis=0), jnp.sum(upstream, axis=0)


def stacked_heads(values):
    lane = lax.broadcasted_iota(jnp.int32, values.shape, 1)
    none = jnp.zeros_like(values)
    return jnp.concatenate(
        [jnp.where(lane < HD, values, none), jnp.where(lane >= HD, values, none)], axis=0
    )


def merged_heads(stacked):
    half = stacked.shape[0] // 2
    lane = lax.broadcasted_iota(jnp.int32, (half, PAIR), 1)
    return jnp.where(lane < HD, stacked[:half], stacked[half:])


def forward_kernel(q_ref, kv_ref, qid_ref, kid_ref, o_ref, total_ref):
    queries = stacked_heads(q_ref[0]) * jnp.asarray(HD**-0.5, LOW)
    scores = right_transposed(queries, kv_ref[0, :, :PAIR])
    qid = qid_ref[0]
    allowed = kid_ref[0] <= jnp.concatenate([qid, qid], axis=0)
    scores = jnp.where(allowed, scores, MASKED)
    highest = jnp.max(scores, axis=-1, keepdims=True)
    exponent = jnp.exp(scores - highest)
    denominator = jnp.sum(exponent, axis=-1, keepdims=True)
    context = product(exponent.astype(LOW), kv_ref[0, :, PAIR:]) / denominator
    o_ref[0] = merged_heads(context).astype(LOW)
    totals = highest + jnp.log(denominator)
    total_ref[0, 0] = jnp.transpose(jnp.broadcast_to(totals, (totals.shape[0], 128)))[:8]


def backward_kernel(q_ref, kv_ref, qid_ref, kid_ref, o_ref, do_ref, total_ref, dq_ref, dkv_ref):
    queries = stacked_heads(q_ref[0]) * jnp.asarray(HD**-0.5, LOW)
    upstream = stacked_heads(do_ref[0])
    both = do_ref[0].astype(WIDE) * o_ref[0].astype(WIDE)
    row = lax.broadcasted_iota(jnp.int32, (8, PAIR), 0)
    lane = lax.broadcasted_iota(jnp.int32, (8, PAIR), 1)
    pick = jnp.where(lane // HD == row, 1.0, 0.0).astype(WIDE)
    inner = lax.dot_general(
        pick,
        both,
        (((1,), (1,)), ((), ())),
        precision=lax.Precision.HIGHEST,
        preferred_element_type=WIDE,
    )
    inner = jnp.concatenate([inner[0:1], inner[1:2]], axis=1)
    keys = kv_ref[0, :, :PAIR]
    qid = qid_ref[0]
    allowed = kid_ref[0] <= jnp.concatenate([qid, qid], axis=1)
    scores = jnp.where(allowed, right_transposed(keys, queries), MASKED)
    weights = jnp.exp(scores - total_ref[0, 0, 0:1])
    dkv_ref[0, :, PAIR:] = product(weights.astype(LOW), upstream).astype(LOW)
    weight_grads = right_transposed(kv_ref[0, :, PAIR:], upstream)
    score_grads = (weights * (weight_grads - inner)).astype(LOW)
    dkv_ref[0, :, :PAIR] = product(score_grads, queries).astype(LOW)
    dq = left_transposed(score_grads, keys) * (HD**-0.5)
    dq_ref[0] = merged_heads(dq).astype(LOW)


def attend_forward(queries, keys_values, ids):
    batch, rows, width = queries.shape
    keys = keys_values.shape[1]
    pairs = width // PAIR
    one = pl.BlockSpec((1, rows, PAIR), lambda b, p: (b, 0, p))
    work = batch * pairs * rows * keys
    return pl.pallas_call(
        forward_kernel,
        grid=(batch, pairs),
        in_specs=[
            one,
            pl.BlockSpec((1, keys, 2 * PAIR), lambda b, p: (b, 0, p)),
            pl.BlockSpec((1, rows, 1), lambda b, p: (b, 0, 0)),
            pl.BlockSpec((1, 1, keys), lambda b, p: (b, 0, 0)),
        ],
        out_specs=[one, pl.BlockSpec((1, 1, 8, 2 * rows), lambda b, p: (b, p, 0, 0))],
        out_shape=[
            jax.ShapeDtypeStruct((batch, rows, width), LOW),
            jax.ShapeDtypeStruct((batch, pairs, 8, 2 * rows), WIDE),
        ],
        cost_estimate=pl.CostEstimate(
            flops=4000 * work, transcendentals=2 * work, bytes_accessed=8 * batch * keys * width
        ),
        name="attend_forward",
    )(queries, keys_values, ids[3], ids[0])


def attend_backward(queries, keys_values, ids, context, upstream, totals, start, count):
    _, rows, width = queries.shape
    keys = keys_values.shape[1]
    pairs = width // PAIR
    one = pl.BlockSpec((1, rows, PAIR), lambda b, p: (start + b, 0, p))
    work = count * pairs * rows * keys
    return pl.pallas_call(
        backward_kernel,
        grid=(count, pairs),
        in_specs=[
            one,
            pl.BlockSpec((1, keys, 2 * PAIR), lambda b, p: (start + b, 0, p)),
            pl.BlockSpec((1, 1, rows), lambda b, p: (start + b, 0, 0)),
            pl.BlockSpec((1, keys, 1), lambda b, p: (start + b, 0, 0)),
            one,
            one,
            pl.BlockSpec((1, 1, 8, 2 * rows), lambda b, p: (start + b, p, 0, 0)),
        ],
        out_specs=[
            pl.BlockSpec((1, rows, PAIR), lambda b, p: (b, 0, p)),
            pl.BlockSpec((1, keys, 2 * PAIR), lambda b, p: (b, 0, p)),
        ],
        out_shape=[
            jax.ShapeDtypeStruct((count, rows, width), LOW),
            jax.ShapeDtypeStruct((count, keys, 2 * width), LOW),
        ],
        cost_estimate=pl.CostEstimate(
            flops=4000 * work, transcendentals=2 * work, bytes_accessed=8 * count * keys * width
        ),
        name="attend_backward",
    )(queries, keys_values, ids[2], ids[1], context, upstream, totals)


CHUNK = 512


def normalised(summed):
    centre = summed - jnp.mean(summed, axis=-1, keepdims=True)
    inverse = lax.rsqrt(jnp.mean(centre * centre, axis=-1, keepdims=True) + EPSILON)
    return centre * inverse, inverse


def normalised_backward(unit, inverse, scaled):
    mean_scaled = jnp.mean(scaled, axis=-1, keepdims=True)
    mean_both = jnp.mean(scaled * unit, axis=-1, keepdims=True)
    return (scaled - mean_scaled - unit * mean_both) * inverse


def gelu_pair(values):
    size = jnp.abs(values) * (0.5**0.5)
    bell = jnp.exp(-0.5 * values * values)
    t = 1.0 / (1.0 + 0.3275911 * size)
    series = t * (
        0.127414796
        + t * (-0.142248368 + t * (0.7107068705 + t * (-0.7265760135 + t * 0.5307027145)))
    )
    tail = series * bell
    below = jnp.where(values >= 0, 1.0 - tail, tail)
    return values * below, below + values * bell * 0.3989422804014327


def total_row(values):
    return jnp.sum(values, axis=0, keepdims=True)


def ffn_kernel(
    first_ref,
    cross_ref,
    cot_ref,
    vector_ref,
    hidden_bias_ref,
    early_ref,
    in_ref,
    out_ref,
    final_ref,
    d_sum_ref,
    d_ctx_ref,
    g_cross_ref,
    sums_ref,
    hidden_sums_ref,
    g_in_ref,
    g_out_ref,
    w_cross,
    w_in,
    w_out,
    hidden,
    slope,
    total,
    low,
    d_low,
    g_in,
    g_out,
    load_sem,
    in_sem,
    out_sem,
):
    rows, width = first_ref.shape
    count = w_in.shape[1] // CHUNK
    cross_at = early_ref.shape[1] - width
    loads = [
        pltpu.make_async_copy(early_ref.at[:, cross_at:], w_cross, load_sem.at[0]),
        pltpu.make_async_copy(in_ref, w_in, load_sem.at[1]),
        pltpu.make_async_copy(out_ref, w_out, load_sem.at[2]),
    ]
    for load in loads:
        load.start()
    loads[0].wait()
    second_sum = first_ref[...] + product(cross_ref[...], w_cross[...]) + vector_ref[0:1]
    unit, inverse = normalised(second_sum)
    second = unit * vector_ref[1:2] + vector_ref[2:3]
    low[...] = second.astype(LOW)
    total[...] = second + vector_ref[3:4]
    d_sum_ref[...] = unit
    loads[1].wait()
    loads[2].wait()

    def forward(step, carry):
        at = pl.ds(pl.multiple_of(step * CHUNK, CHUNK), CHUNK)
        activation = product(low[...], w_in[:, at]) + hidden_bias_ref[:, at]
        value, slope_value = gelu_pair(activation)
        value = value.astype(LOW)
        hidden[:, at] = value
        slope[:, at] = slope_value
        total[...] += product(value, w_out[at, :])
        return carry

    lax.fori_loop(0, count, forward, 0)
    third, third_inverse = normalised(total[...])
    final_ref[...] = (third * vector_ref[4:5] + vector_ref[5:6]).astype(LOW)
    upstream = cot_ref[...].astype(WIDE)
    sums_ref[0:1] = total_row(upstream * third)
    sums_ref[1:2] = total_row(upstream)
    d_third = normalised_backward(third, third_inverse, upstream * vector_ref[4:5])
    d_low[...] = d_third.astype(LOW)
    sums_ref[2:3] = total_row(d_low[...].astype(WIDE))
    total[...] = d_third

    def copies(step):
        at = pl.ds(pl.multiple_of(step * CHUNK, CHUNK), CHUNK)
        return (
            pltpu.make_async_copy(g_in.at[:, at], g_in_ref.at[:, at], in_sem.at[step]),
            pltpu.make_async_copy(g_out.at[at, :], g_out_ref.at[at, :], out_sem.at[step]),
        )

    def backward(step, carry):
        at = pl.ds(pl.multiple_of(step * CHUNK, CHUNK), CHUNK)
        g_out[at, :] = left_transposed(hidden[:, at], d_low[...]).astype(LOW)
        d_hidden = right_transposed(d_low[...], w_out[at, :])
        d_activation = (d_hidden * slope[:, at]).astype(LOW)
        hidden_sums_ref[:, at] = total_row(d_activation.astype(WIDE))
        g_in[:, at] = left_transposed(low[...], d_activation).astype(LOW)
        total[...] += right_transposed(d_activation, w_in[:, at])
        for copy in copies(step):
            copy.start()
        return carry

    lax.fori_loop(0, count, backward, 0)
    d_second = total[...]
    unit = d_sum_ref[...]
    sums_ref[3:4] = total_row(d_second * unit)
    sums_ref[4:5] = total_row(d_second)
    d_second_sum = normalised_backward(unit, inverse, d_second * vector_ref[1:2])
    d_sum_ref[...] = d_second_sum
    d_cross = d_second_sum.astype(LOW)
    sums_ref[5:6] = total_row(d_cross.astype(WIDE))
    d_ctx = right_transposed(d_cross, w_cross[...]).astype(LOW)
    d_ctx_ref[...] = d_ctx
    sums_ref[6:7] = total_row(d_ctx.astype(WIDE))
    sums_ref[7:8] = jnp.zeros_like(sums_ref[7:8])
    g_cross_ref[...] = left_transposed(cross_ref[...], d_cross).astype(LOW)

    def drain(step, carry):
        for copy in copies(step):
            copy.wait()
        return carry

    lax.fori_loop(0, count, drain, 0)


def ffn_stage(first, cross, cotangent, vectors, hidden_bias, early, ffn_in, ffn_out):
    rows, width = first.shape
    hidden_width = ffn_in.shape[1]
    count = hidden_width // CHUNK
    inside = pl.BlockSpec(memory_space=pltpu.VMEM)
    outside = pl.BlockSpec(memory_space=pl.ANY)
    return pl.pallas_call(
        ffn_kernel,
        in_specs=[inside] * 5 + [outside] * 3,
        out_specs=[inside] * 6 + [outside] * 2,
        out_shape=[
            jax.ShapeDtypeStruct((rows, width), LOW),
            jax.ShapeDtypeStruct((rows, width), WIDE),
            jax.ShapeDtypeStruct((rows, width), LOW),
            jax.ShapeDtypeStruct((width, width), LOW),
            jax.ShapeDtypeStruct((8, width), WIDE),
            jax.ShapeDtypeStruct((1, hidden_width), WIDE),
            jax.ShapeDtypeStruct((width, hidden_width), LOW),
            jax.ShapeDtypeStruct((hidden_width, width), LOW),
        ],
        scratch_shapes=[
            pltpu.VMEM((width, width), LOW),
            pltpu.VMEM((width, hidden_width), LOW),
            pltpu.VMEM((hidden_width, width), LOW),
            pltpu.VMEM((rows, hidden_width), LOW),
            pltpu.VMEM((rows, hidden_width), WIDE),
            pltpu.VMEM((rows, width), WIDE),
            pltpu.VMEM((rows, width), LOW),
            pltpu.VMEM((rows, width), LOW),
            pltpu.VMEM((width, hidden_width), LOW),
            pltpu.VMEM((hidden_width, width), LOW),
            pltpu.SemaphoreType.DMA((3,)),
            pltpu.SemaphoreType.DMA((count,)),
            pltpu.SemaphoreType.DMA((count,)),
        ],
        compiler_params=pltpu.CompilerParams(vmem_limit_bytes=58 << 20),
        cost_estimate=pl.CostEstimate(
            flops=16 * rows * width * hidden_width,
            transcendentals=rows * hidden_width,
            bytes_accessed=12 * width * hidden_width,
        ),
        name="ffn_stage",
    )(first, cross, cotangent, vectors, hidden_bias, early, ffn_in, ffn_out)


def gathered_back(own, groups):
    place = lax.axis_index("seq")
    behind = lax.ppermute(own, "seq", [(source, source + 1) for source in range(groups - 1)])
    ahead = lax.ppermute(own, "seq", [(source, source - 1) for source in range(1, groups)])
    if groups == 4:
        last = lax.ppermute(own, "seq", [(0, 3)])
        going = jnp.where(place == 2, behind, own)
        slots = [own, behind, lax.ppermute(going, "seq", [(0, 2), (2, 3)])]
    else:
        slots = [own, behind]
        for step in range(2, groups):
            pairs = [(source, source + 1) for source in range(step - 1, groups - 1)]
            slots.append(lax.ppermute(slots[-1], "seq", pairs))
        last = slots.pop()
    return slots + [jnp.where(place == groups - 1, last, ahead)]


def scatter_steps(slots, groups):
    forth = [(source, source + 1) for source in range(groups - 1)]
    if groups == 4:
        ahead = lax.ppermute(slots[2], "seq", [(3, 2)])
        parts = [
            lax.ppermute(slots[3], "seq", [(3, 0)]),
            lax.ppermute(slots[2], "seq", [(2, 0)]),
            lax.ppermute(slots[3], "seq", forth),
        ]
        ahead, parts = yield ahead, parts
        back = [(source, source - 1) for source in range(1, groups)]
        last, parts = yield lax.ppermute(plus(slots[1], ahead), "seq", back), parts
        parts = parts + [last]
    else:
        parts = [lax.ppermute(slots[groups - 1], "seq", forth)]
        for step in range(groups - 1, 0, -1):
            pairs = [(source, source - step) for source in range(step, groups)]
            parts.append(lax.ppermute(slots[step], "seq", pairs))
        parts = yield parts
    return sum([part.astype(WIDE) for part in parts], slots[0].astype(WIDE))


def tied(value, *others):
    return lax.optimization_barrier((value,) + others)[0]


def by_bit(bit, own, other, axis=0):
    own, other = jnp.expand_dims(own, axis), jnp.expand_dims(other, axis)
    return jnp.where(
        bit == 0,
        jnp.concatenate([own, other], axis=axis),
        jnp.concatenate([other, own], axis=axis),
    )


def crossed(value, axis_name, masks):
    count = lax.axis_size(axis_name)
    pairs = [(source, source ^ masks[source % len(masks)]) for source in range(count)]
    return lax.ppermute(value, axis_name, pairs)


CORE = (1,)
FIRST = (2, 4)
SECOND = (4, 2)


def chip_masks(core):
    first = jnp.where(core == 0, 1, 2)
    return first, 3 - first


def gather_rows(shard):
    return lax.all_gather(shard, "dp", axis=0, tiled=True)


def picked(values, position, axis=0):
    return lax.dynamic_index_in_dim(values, position, axis, keepdims=False)


def plus(left, right):
    return (left.astype(WIDE) + right.astype(WIDE)).astype(LOW)


class Chain:
    def __init__(self, steps):
        self.steps = steps
        self.pending = next(steps)
        self.result = None

    def step(self):
        if self.result is None:
            try:
                self.pending = self.steps.send(self.pending)
            except StopIteration as stop:
                self.result = stop.value


def pumped(values, *chains):
    live = [chain for chain in chains if chain.result is None]
    values, arrived = lax.optimization_barrier((values, [chain.pending for chain in live]))
    for chain, brought in zip(live, arrived):
        chain.pending = brought
        chain.step()
    return values


def finished(*chains):
    while any(chain.result is None for chain in chains):
        for chain in chains:
            chain.step()
    return [chain.result for chain in chains]


def places_steps(sums):
    place = lax.axis_index("seq")
    sums = plus(sums, (yield lax.ppermute(sums, "seq", [(0, 1), (3, 2)])))
    sums = plus(sums, (yield lax.ppermute(sums, "seq", [(1, 2), (2, 1)])))
    back = yield lax.ppermute(sums, "seq", [(1, 0), (2, 3)])
    return jnp.where((place == 0) | (place == 3), back, sums)


def offloaded_steps(gradient):
    share = yield lax.psum_scatter(gradient, "dp", scatter_dimension=0, tiled=True)
    if lax.axis_size("dp") != 8 or lax.axis_size("seq") != 4:
        return (yield lax.psum(share, "seq")).astype(WIDE)
    return (yield from places_steps(share)).astype(WIDE)


def exchange_steps(gradient):
    if lax.axis_size("dp") != 8 or lax.axis_size("seq") != 4:
        return (yield from offloaded_steps(gradient))
    index = lax.axis_index("dp")
    core, chip = index % 2, index // 2
    first, second = chip_masks(core)
    rows, columns = gradient.shape
    half = rows // 16
    view = gradient.reshape(4, 2, 2, half, columns)
    sums = plus(picked(view, core, 2), (yield crossed(picked(view, 1 - core, 2), "dp", CORE)))
    going = jnp.stack([picked(sums, chip ^ first), picked(sums, chip ^ 3)])
    kept = jnp.stack([picked(sums, chip), picked(sums, chip ^ second)])
    sums = plus(kept, (yield crossed(going, "dp", FIRST)))
    sums = plus(sums[0], (yield crossed(sums[1], "dp", SECOND)))
    sums = yield from places_steps(sums)
    own = by_bit(core, picked(sums, core), (yield crossed(picked(sums, 1 - core), "dp", CORE)))
    return own.reshape(2 * half, columns).astype(WIDE)


def gather_small(values):
    if lax.axis_size("dp") != 8:
        return lax.all_gather(values, "dp", axis=0)
    index = lax.axis_index("dp")
    out = by_bit(index % 2, values, crossed(values, "dp", CORE))
    out = by_bit(index // 2 % 2, out, crossed(out, "dp", (2,)))
    out = by_bit(index // 4, out, crossed(out, "dp", (4,)))
    return out.reshape((8,) + values.shape)


def small_steps(values):
    if lax.axis_size("dp") != 8 or lax.axis_size("seq") != 4:
        return (yield lax.psum(values, ("dp", "seq")))
    for axis_name, mask in (("dp", 1), ("dp", 2), ("dp", 4), ("seq", 1), ("seq", 2)):
        values = values + (yield crossed(values, axis_name, (mask,)))
    return values


def gather_steps(values):
    if lax.axis_size("seq") != 4:
        return (yield lax.all_gather(values, "seq", axis=0))
    place = lax.axis_index("seq")
    out = by_bit(place % 2, values, (yield crossed(values, "seq", (1,))))
    out = by_bit(place // 2, out, (yield crossed(out, "seq", (2,))))
    return out.reshape((4,) + values.shape)


def chunk_steps(values):
    if lax.axis_size("seq") != 4:
        return (yield lax.psum_scatter(values, "seq", scatter_dimension=0, tiled=False)).astype(WIDE)
    place = lax.axis_index("seq")
    low_bit, high_bit = place % 2, place // 2
    values = values.reshape((2, 2) + values.shape[1:])
    going = picked(values, 1 - low_bit, 1)
    values = plus(picked(values, low_bit, 1), (yield crossed(going, "seq", (1,))))
    going = picked(values, 1 - high_bit)
    return picked(values, high_bit).astype(WIDE) + (yield crossed(going, "seq", (2,))).astype(WIDE)


def interleaved(keys_values):
    rows, columns = keys_values.shape
    view = keys_values.reshape(rows, 2, columns // (2 * PAIR), PAIR)
    return view.transpose(0, 2, 1, 3).reshape(rows, columns)


def deinterleaved(keys_values):
    rows, columns = keys_values.shape
    view = keys_values.reshape(rows, columns // (2 * PAIR), 2, PAIR)
    return view.transpose(0, 2, 1, 3).reshape(rows, columns)


def local(
    tokens,
    encoded,
    cotangent,
    attn_in,
    attn_out,
    cross_in,
    cross_out,
    ffn_in,
    ffn_out,
    gains,
    biases,
    bias_ff,
    block_ids,
    enc_lengths,
):
    groups = lax.axis_size("seq")
    shards = lax.axis_size("dp")
    place = lax.axis_index("seq")
    owner = lax.axis_index("dp")
    batch, local_len, width = tokens.shape
    enc_local = encoded.shape[1]
    rows = batch * local_len
    length = local_len * groups
    enc_length = enc_local * groups
    hidden_width = ffn_in.shape[1]

    attn_q, attn_kv = attn_in[:, :width], interleaved(attn_in[:, width:])
    cross_q, cross_kv = cross_in[:, :width], interleaved(cross_in[:, width:])
    early = gather_rows(
        jnp.concatenate([attn_q, attn_kv, attn_out, cross_q, cross_kv, cross_out], axis=1)
    )
    slots = gathered_back(tokens, groups)
    small = jnp.concatenate([gains, biases, bias_ff.reshape(-1, gains.shape[1])], axis=0)
    small = gather_small(small)
    small = small.astype(WIDE)
    gain_rows = gains.shape[0]
    bias_rows = biases.shape[0]
    vectors = small[:, : gain_rows + bias_rows].transpose(1, 0, 2).reshape(-1, width)
    gain_all = vectors[:gain_rows]
    bias_all = vectors[gain_rows:]
    bias_hidden = small[:, gain_rows + bias_rows :].reshape(hidden_width)
    blank = jnp.zeros((width,), WIDE)
    value_bias = interleaved(jnp.concatenate([blank, bias_all[1]])[None])
    cross_value_bias = interleaved(jnp.concatenate([blank, bias_all[4]])[None])

    chunks = block_ids.reshape(batch, groups, local_len)
    order = (place - jnp.arange(groups)) % groups
    kid = jnp.take(chunks, order, axis=1).reshape(batch, length)
    qid = kid[:, :local_len]
    enc_kid = jnp.broadcast_to(jnp.arange(enc_length, dtype=jnp.int32)[None], (batch, enc_length))
    enc_qid = jnp.broadcast_to(enc_lengths[:, None] - 1, (batch, local_len))
    ids = (kid[:, None, :], kid[:, :, None], qid[:, None, :], qid[:, :, None])
    enc_ids = (enc_kid[:, None, :], enc_kid[:, :, None], enc_qid[:, None, :], enc_qid[:, :, None])

    vectors = (gain_all, bias_all, bias_hidden, value_bias, cross_value_bias)
    early, slots, vectors, ids, enc_ids = lax.optimization_barrier(
        (early, slots, vectors, ids, enc_ids)
    )
    gain_all, bias_all, bias_hidden, value_bias, cross_value_bias = vectors
    attn_q, attn_kv = early[:, :width], early[:, width : 3 * width]
    attn_out, cross_q = early[:, 3 * width : 4 * width], early[:, 4 * width : 5 * width]
    cross_kv = early[:, 5 * width : 7 * width]
    ffn_in = gather_rows(ffn_in)
    ffn_out = gather_rows(ffn_out)
    enc_gather = Chain(gather_steps(tied(encoded, slots[-1])))

    token_all = jnp.concatenate(slots, axis=1).reshape(batch * length, width)
    token_flat = tokens.reshape(rows, width)
    queries = (product(token_flat, attn_q) + bias_all[0]).astype(LOW)
    queries = queries.reshape(batch, local_len, width)
    keys_values = (product(token_all, attn_kv) + value_bias).astype(LOW)
    keys_values = keys_values.reshape(batch, length, 2 * width)

    queries, keys_values = pumped((queries, keys_values), enc_gather)
    context, totals = attend_forward(queries, keys_values, ids)
    context = pumped(context, enc_gather)
    encoded = enc_gather.result
    enc_all = encoded.transpose(1, 0, 2, 3).reshape(batch * enc_length, width)
    enc_kv = (product(enc_all, cross_kv) + cross_value_bias).astype(LOW)
    enc_kv = enc_kv.reshape(batch, enc_length, 2 * width)
    context_flat = context.reshape(rows, width)
    first_sum = token_flat.astype(WIDE) + product(context_flat, attn_out) + bias_all[2]
    first = layer_norm(first_sum, gain_all[0], bias_all[7])
    first_low = first.astype(LOW)
    cross_queries = (product(first_low, cross_q) + bias_all[3]).astype(LOW)
    cross_queries = cross_queries.reshape(batch, local_len, width)
    cross_context, cross_totals = attend_forward(cross_queries, enc_kv, enc_ids)
    cross_flat = cross_context.reshape(rows, width)
    stage_vectors = jnp.stack(
        [bias_all[5], gain_all[1], bias_all[8], bias_all[6], gain_all[2], bias_all[9]]
    )
    final, d_second_sum, d_cross_ctx, grad_cross_out, sums, d_bias_hidden, grad_in, grad_out = (
        ffn_stage(
            first,
            cross_flat,
            cotangent.reshape(rows, width),
            stage_vectors,
            bias_hidden[None],
            early,
            ffn_in,
            ffn_out,
        )
    )
    out_chain = Chain(offloaded_steps(grad_out))
    in_chain = Chain(offloaded_steps(grad_in))
    d_cross_ctx = d_cross_ctx.reshape(cross_context.shape)
    d_cross_q, d_enc = attend_backward(
        cross_queries, enc_kv, enc_ids, cross_context, d_cross_ctx, cross_totals, 0, batch
    )
    d_cross_q = d_cross_q.reshape(rows, width)
    d_enc = d_enc.reshape(-1, 2 * width)
    d_first = d_second_sum + right_transposed(d_cross_q, cross_q)
    d_first_sum, d_gain_one, d_offset_one = norm_backward(first_sum, gain_all[0], d_first)
    d_attn = d_first_sum.astype(LOW)
    d_context = right_transposed(d_attn, attn_out).astype(LOW).reshape(context.shape)

    def attention_backward(number, d_context):
        d_q, d_kv = attend_backward(
            queries, keys_values, ids, context, d_context, totals, number, 1
        )
        d_part = right_transposed(d_kv[0], attn_kv).astype(LOW)
        d_part = d_part.reshape(groups, local_len, width)
        return d_q, d_kv, Chain(scatter_steps(list(d_part), groups))

    d_queries, d_keys_values, token_chains = [], [], []
    for number in range(batch):
        d_q, d_kv, chain = attention_backward(number, d_context)
        d_queries.append(d_q)
        d_keys_values.append(d_kv)
        token_chains.append(chain)
        if number == 0:
            left = (context_flat, first_low, enc_all, d_attn, d_cross_q, d_enc)
            left, d_kv = lax.optimization_barrier((left, d_kv))
            middle = [left_transposed(one, two) for one, two in zip(left[:3], left[3:])]
            middle.append(grad_cross_out)
            middle = jnp.concatenate([part.astype(LOW) for part in middle], axis=1)
            mid_chain = Chain(exchange_steps(middle))
            d_encoded = right_transposed(left[5], cross_kv)
            d_encoded = d_encoded.reshape(batch, groups, enc_local, width).astype(LOW)
            enc_chain = Chain(chunk_steps(d_encoded.transpose(1, 0, 2, 3)))
            d_context, middle, d_encoded = lax.optimization_barrier((d_context, middle, d_encoded))
    d_query = jnp.concatenate(d_queries, axis=0).reshape(rows, width)
    d_kv = jnp.concatenate(d_keys_values, axis=0).reshape(batch * length, 2 * width)
    d_query, d_kv = pumped((d_query, d_kv), mid_chain, enc_chain, token_chains[0])
    grad_attn = jnp.concatenate(
        [
            left_transposed(token_flat, d_query).astype(LOW),
            left_transposed(token_all, d_kv).astype(LOW),
        ],
        axis=1,
    )
    attn_chain = Chain(exchange_steps(grad_attn))
    d_tokens = d_first_sum + right_transposed(d_query, attn_q)
    d_tokens = d_tokens.reshape(tokens.shape)
    vector_grads = jnp.stack(
        [
            d_gain_one,
            sums[3],
            sums[0],
            column_total(d_query),
            column_total(d_context.reshape(rows, width)),
            column_total(d_attn),
            column_total(d_cross_q),
            sums[6],
            sums[5],
            sums[2],
            d_offset_one,
            sums[4],
            sums[1],
        ]
    )
    vector_grads = jnp.concatenate([vector_grads, d_bias_hidden.reshape(-1, width)], axis=0)
    small_chain = Chain(small_steps(vector_grads))
    chains = [attn_chain, small_chain, mid_chain, out_chain, enc_chain, in_chain]
    grad_attn, vector_grads, middle, grad_ffn_out, d_encoded, grad_ffn_in, *d_parts = finished(
        *chains, *token_chains
    )
    d_tokens = jnp.stack([d_tokens[number] + part for number, part in enumerate(d_parts)])
    grad_attn_in = jnp.concatenate(
        [grad_attn[:, :width], deinterleaved(grad_attn[:, width:])], axis=1
    )
    grad_cross_in = jnp.concatenate(
        [middle[:, width : 2 * width], deinterleaved(middle[:, 2 * width : 4 * width])], axis=1
    )
    flat_hidden = vector_grads[gain_rows + bias_rows :].reshape(-1)
    part = width // shards
    mine = lax.dynamic_slice_in_dim(vector_grads, owner * part, part, axis=1)
    hidden_part = hidden_width // shards
    grad_bias_ff = lax.dynamic_slice_in_dim(flat_hidden, owner * hidden_part, hidden_part)
    return (
        final.reshape(batch, local_len, width),
        d_tokens,
        d_encoded,
        grad_attn_in,
        middle[:, :width],
        grad_cross_in,
        middle[:, 4 * width :],
        grad_ffn_in,
        grad_ffn_out,
        mine[:gain_rows],
        mine[gain_rows : gain_rows + bias_rows],
        grad_bias_ff,
    )


def solution(mesh):
    split = P("dp", "seq", None)
    rows = P("dp", None)
    columns = P(None, "dp")
    vector = P("dp")
    in_specs = (split,) * 3 + (rows,) * 6 + (columns, columns, vector, rows, vector)
    out_specs = (split,) * 3 + (rows,) * 6 + (columns, columns, vector)
    return jax.shard_map(local, mesh=mesh, in_specs=in_specs, out_specs=out_specs, check_vma=False)
```

```python
import jax
import jax.numpy as jnp
from jax import lax
from jax.experimental import pallas as pl
from jax.experimental.pallas import tpu as pltpu
from jax.sharding import PartitionSpec as P

HD = 64
PAIR = 2 * HD
EPSILON = 1e-05
MASKED = -1e30
LOW = jnp.bfloat16
WIDE = jnp.float32


def product(left, right):
    return jnp.dot(left, right, preferred_element_type=WIDE)


def left_transposed(left, right):
    return lax.dot_general(left, right, (((0,), (0,)), ((), ())), preferred_element_type=WIDE)


def right_transposed(left, right):
    return lax.dot_general(left, right, (((1,), (1,)), ((), ())), preferred_element_type=WIDE)


def column_total(values):
    return jnp.sum(values.astype(WIDE), axis=0)


def layer_norm(summed, gain, offset):
    centre = summed - jnp.mean(summed, axis=-1, keepdims=True)
    spread = jnp.mean(centre * centre, axis=-1, keepdims=True)
    return centre * lax.rsqrt(spread + EPSILON) * gain + offset


def norm_backward(summed, gain, upstream):
    centre = summed - jnp.mean(summed, axis=-1, keepdims=True)
    spread = jnp.mean(centre * centre, axis=-1, keepdims=True)
    inverse = lax.rsqrt(spread + EPSILON)
    unit = centre * inverse
    scaled = upstream * gain
    mean_scaled = jnp.mean(scaled, axis=-1, keepdims=True)
    mean_both = jnp.mean(scaled * unit, axis=-1, keepdims=True)
    d_summed = (scaled - mean_scaled - unit * mean_both) * inverse
    return d_summed, jnp.sum(upstream * unit, axis=0), jnp.sum(upstream, axis=0)


def stacked_heads(values):
    lane = lax.broadcasted_iota(jnp.int32, values.shape, 1)
    none = jnp.zeros_like(values)
    return jnp.concatenate(
        [jnp.where(lane < HD, values, none), jnp.where(lane >= HD, values, none)], axis=0
    )


def merged_heads(stacked):
    half = stacked.shape[0] // 2
    lane = lax.broadcasted_iota(jnp.int32, (half, PAIR), 1)
    return jnp.where(lane < HD, stacked[:half], stacked[half:])


def forward_kernel(q_ref, kv_ref, qid_ref, kid_ref, o_ref, total_ref):
    queries = stacked_heads(q_ref[0]) * jnp.asarray(HD**-0.5, LOW)
    scores = right_transposed(queries, kv_ref[0, :, :PAIR])
    qid = qid_ref[0]
    allowed = kid_ref[0] <= jnp.concatenate([qid, qid], axis=0)
    scores = jnp.where(allowed, scores, MASKED)
    highest = jnp.max(scores, axis=-1, keepdims=True)
    exponent = jnp.exp(scores - highest)
    denominator = jnp.sum(exponent, axis=-1, keepdims=True)
    context = product(exponent.astype(LOW), kv_ref[0, :, PAIR:]) / denominator
    o_ref[0] = merged_heads(context).astype(LOW)
    totals = highest + jnp.log(denominator)
    total_ref[0, 0] = jnp.transpose(jnp.broadcast_to(totals, (totals.shape[0], 128)))[:8]


def backward_kernel(q_ref, kv_ref, qid_ref, kid_ref, o_ref, do_ref, total_ref, dq_ref, dkv_ref):
    queries = stacked_heads(q_ref[0]) * jnp.asarray(HD**-0.5, LOW)
    upstream = stacked_heads(do_ref[0])
    both = do_ref[0].astype(WIDE) * o_ref[0].astype(WIDE)
    row = lax.broadcasted_iota(jnp.int32, (8, PAIR), 0)
    lane = lax.broadcasted_iota(jnp.int32, (8, PAIR), 1)
    pick = jnp.where(lane // HD == row, 1.0, 0.0).astype(WIDE)
    inner = lax.dot_general(
        pick,
        both,
        (((1,), (1,)), ((), ())),
        precision=lax.Precision.HIGHEST,
        preferred_element_type=WIDE,
    )
    inner = jnp.concatenate([inner[0:1], inner[1:2]], axis=1)
    keys = kv_ref[0, :, :PAIR]
    qid = qid_ref[0]
    allowed = kid_ref[0] <= jnp.concatenate([qid, qid], axis=1)
    scores = jnp.where(allowed, right_transposed(keys, queries), MASKED)
    weights = jnp.exp(scores - total_ref[0, 0, 0:1])
    dkv_ref[0, :, PAIR:] = product(weights.astype(LOW), upstream).astype(LOW)
    weight_grads = right_transposed(kv_ref[0, :, PAIR:], upstream)
    score_grads = (weights * (weight_grads - inner)).astype(LOW)
    dkv_ref[0, :, :PAIR] = product(score_grads, queries).astype(LOW)
    dq = left_transposed(score_grads, keys) * (HD**-0.5)
    dq_ref[0] = merged_heads(dq).astype(LOW)


def attend_forward(queries, keys_values, ids):
    batch, rows, width = queries.shape
    keys = keys_values.shape[1]
    pairs = width // PAIR
    one = pl.BlockSpec((1, rows, PAIR), lambda b, p: (b, 0, p))
    work = batch * pairs * rows * keys
    return pl.pallas_call(
        forward_kernel,
        grid=(batch, pairs),
        in_specs=[
            one,
            pl.BlockSpec((1, keys, 2 * PAIR), lambda b, p: (b, 0, p)),
            pl.BlockSpec((1, rows, 1), lambda b, p: (b, 0, 0)),
            pl.BlockSpec((1, 1, keys), lambda b, p: (b, 0, 0)),
        ],
        out_specs=[one, pl.BlockSpec((1, 1, 8, 2 * rows), lambda b, p: (b, p, 0, 0))],
        out_shape=[
            jax.ShapeDtypeStruct((batch, rows, width), LOW),
            jax.ShapeDtypeStruct((batch, pairs, 8, 2 * rows), WIDE),
        ],
        cost_estimate=pl.CostEstimate(
            flops=4000 * work, transcendentals=2 * work, bytes_accessed=8 * batch * keys * width
        ),
        name="attend_forward",
    )(queries, keys_values, ids[3], ids[0])


def attend_backward(queries, keys_values, ids, context, upstream, totals, start, count):
    _, rows, width = queries.shape
    keys = keys_values.shape[1]
    pairs = width // PAIR
    one = pl.BlockSpec((1, rows, PAIR), lambda b, p: (start + b, 0, p))
    work = count * pairs * rows * keys
    return pl.pallas_call(
        backward_kernel,
        grid=(count, pairs),
        in_specs=[
            one,
            pl.BlockSpec((1, keys, 2 * PAIR), lambda b, p: (start + b, 0, p)),
            pl.BlockSpec((1, 1, rows), lambda b, p: (start + b, 0, 0)),
            pl.BlockSpec((1, keys, 1), lambda b, p: (start + b, 0, 0)),
            one,
            one,
            pl.BlockSpec((1, 1, 8, 2 * rows), lambda b, p: (start + b, p, 0, 0)),
        ],
        out_specs=[
            pl.BlockSpec((1, rows, PAIR), lambda b, p: (b, 0, p)),
            pl.BlockSpec((1, keys, 2 * PAIR), lambda b, p: (b, 0, p)),
        ],
        out_shape=[
            jax.ShapeDtypeStruct((count, rows, width), LOW),
            jax.ShapeDtypeStruct((count, keys, 2 * width), LOW),
        ],
        cost_estimate=pl.CostEstimate(
            flops=4000 * work, transcendentals=2 * work, bytes_accessed=8 * count * keys * width
        ),
        name="attend_backward",
    )(queries, keys_values, ids[2], ids[1], context, upstream, totals)


CHUNK = 768


def normalised(summed):
    centre = summed - jnp.mean(summed, axis=-1, keepdims=True)
    inverse = lax.rsqrt(jnp.mean(centre * centre, axis=-1, keepdims=True) + EPSILON)
    return centre * inverse, inverse


def normalised_backward(unit, inverse, scaled):
    mean_scaled = jnp.mean(scaled, axis=-1, keepdims=True)
    mean_both = jnp.mean(scaled * unit, axis=-1, keepdims=True)
    return (scaled - mean_scaled - unit * mean_both) * inverse


def gelu_pair(values):
    size = jnp.abs(values) * (0.5**0.5)
    bell = jnp.exp(-0.5 * values * values)
    t = 1.0 / (1.0 + 0.3275911 * size)
    series = t * (
        0.127414796
        + t * (-0.142248368 + t * (0.7107068705 + t * (-0.7265760135 + t * 0.5307027145)))
    )
    tail = series * bell
    below = jnp.where(values >= 0, 1.0 - tail, tail)
    return values * below, below + values * bell * 0.3989422804014327


def total_row(values):
    return jnp.sum(values, axis=0, keepdims=True)


def slot_copies(source, keep_ref, send_ref, place_ref, semaphores, columns=None, chips=None):
    rows = keep_ref.shape[1]
    core = place_ref[0]
    found = []
    for chip in range(4) if chips is None else chips:
        for number, (slots_ref, owner) in enumerate(((keep_ref, core), (send_ref, 1 - core))):
            at = pl.ds(pl.multiple_of((2 * chip + owner) * rows, 16), rows)
            slot = place_ref[1 + 4 * number + chip]
            taken, given = source.at[at], slots_ref.at[slot]
            if columns is not None:
                taken, given = source.at[at, columns], slots_ref.at[slot, :, columns]
            found.append(pltpu.make_async_copy(taken, given, semaphores.at[2 * chip + number]))
    return found


def ffn_kernel(
    place_ref,
    first_ref,
    cross_ref,
    cot_ref,
    vector_ref,
    hidden_bias_ref,
    early_ref,
    in_ref,
    out_ref,
    final_ref,
    d_sum_ref,
    d_ctx_ref,
    sums_ref,
    hidden_sums_ref,
    *others,
):
    grad_refs, scratch = others[:-14], others[-14:]
    w_cross, w_in, w_out, hidden, slope, total, low, d_low, g_in, g_out = scratch[:10]
    load_sem, out_sem, in_sem, cross_sem = scratch[10:14]
    rows, width = first_ref.shape
    hidden_width = w_in.shape[1]
    count = hidden_width // CHUNK
    slotted = len(grad_refs) == 4
    cross_at = early_ref.shape[1] - width
    loads = [
        pltpu.make_async_copy(early_ref.at[:, cross_at:], w_cross, load_sem.at[0]),
        pltpu.make_async_copy(in_ref, w_in, load_sem.at[1]),
        pltpu.make_async_copy(out_ref, w_out, load_sem.at[2]),
    ]
    for load in loads:
        load.start()
    loads[0].wait()
    second_sum = first_ref[...] + product(cross_ref[...], w_cross[...]) + vector_ref[0:1]
    unit, inverse = normalised(second_sum)
    second = unit * vector_ref[1:2] + vector_ref[2:3]
    low[...] = second.astype(LOW)
    total[...] = second + vector_ref[3:4]
    d_sum_ref[...] = unit
    loads[1].wait()
    loads[2].wait()

    def forward(step, carry):
        at = pl.ds(pl.multiple_of(step * CHUNK, CHUNK), CHUNK)
        activation = product(low[...], w_in[:, at]) + hidden_bias_ref[:, at]
        value, slope_value = gelu_pair(activation)
        value = value.astype(LOW)
        hidden[:, at] = value
        slope[:, at] = slope_value
        total[...] += product(value, w_out[at, :])
        return carry

    lax.fori_loop(0, count, forward, 0)
    third, third_inverse = normalised(total[...])
    final_ref[...] = (third * vector_ref[4:5] + vector_ref[5:6]).astype(LOW)
    upstream = cot_ref[...].astype(WIDE)
    sums_ref[0:1] = total_row(upstream * third)
    sums_ref[1:2] = total_row(upstream)
    d_third = normalised_backward(third, third_inverse, upstream * vector_ref[4:5])
    d_low[...] = d_third.astype(LOW)
    sums_ref[2:3] = total_row(d_low[...].astype(WIDE))
    total[...] = d_third

    def backward(step, carry):
        at = pl.ds(pl.multiple_of(step * CHUNK, CHUNK), CHUNK)
        g_out[at, :] = left_transposed(hidden[:, at], d_low[...]).astype(LOW)
        d_hidden = right_transposed(d_low[...], w_out[at, :])
        d_activation = (d_hidden * slope[:, at]).astype(LOW)
        hidden_sums_ref[:, at] = total_row(d_activation.astype(WIDE))
        g_in[:, at] = left_transposed(low[...], d_activation).astype(LOW)
        total[...] += right_transposed(d_activation, w_in[:, at])
        if slotted:
            for copy in slot_copies(g_out, *grad_refs[2:], place_ref, out_sem, None, [step]):
                copy.start()
        return carry

    lax.fori_loop(0, count, backward, 0)
    if slotted:
        copies = [
            slot_copies(g_out, *grad_refs[2:], place_ref, out_sem),
            slot_copies(
                g_in, *grad_refs[:2], place_ref, in_sem, pl.ds(0, hidden_width)
            ),
            slot_copies(
                g_in, *grad_refs[:2], place_ref, cross_sem, pl.ds(hidden_width, width)
            ),
        ]
    else:
        copies = [
            [pltpu.make_async_copy(g_out, grad_refs[1], out_sem.at[0])],
            [pltpu.make_async_copy(g_in, grad_refs[0], in_sem.at[0])],
        ]
        copies[0][0].start()
    if slotted:
        for copy in copies[1]:
            copy.start()
    d_second = total[...]
    unit = d_sum_ref[...]
    sums_ref[3:4] = total_row(d_second * unit)
    sums_ref[4:5] = total_row(d_second)
    d_second_sum = normalised_backward(unit, inverse, d_second * vector_ref[1:2])
    d_sum_ref[...] = d_second_sum
    d_cross = d_second_sum.astype(LOW)
    sums_ref[5:6] = total_row(d_cross.astype(WIDE))
    g_in[:, hidden_width:] = left_transposed(cross_ref[...], d_cross).astype(LOW)
    for copy in copies[-1]:
        copy.start()
    d_ctx = right_transposed(d_cross, w_cross[...]).astype(LOW)
    d_ctx_ref[...] = d_ctx
    sums_ref[6:7] = total_row(d_ctx.astype(WIDE))
    sums_ref[7:8] = jnp.zeros_like(sums_ref[7:8])
    for group in copies:
        for copy in group:
            copy.wait()


def ffn_stage(
    places, first, cross, cotangent, vectors, hidden_bias, early, ffn_in, ffn_out, slotted
):
    rows, width = first.shape
    hidden_width = ffn_in.shape[1]
    count = hidden_width // CHUNK
    inside = pl.BlockSpec(memory_space=pltpu.VMEM)
    outside = pl.BlockSpec(memory_space=pl.ANY)
    grads = [(width, hidden_width + width), (hidden_width, width)]
    if slotted:
        grads = [(4, shape[0] // 8, shape[1]) for shape in grads for _ in range(2)]
    return pl.pallas_call(
        ffn_kernel,
        in_specs=[pl.BlockSpec(memory_space=pltpu.SMEM)] + [inside] * 5 + [outside] * 3,
        out_specs=[inside] * 5 + [outside] * len(grads),
        out_shape=[
            jax.ShapeDtypeStruct((rows, width), LOW),
            jax.ShapeDtypeStruct((rows, width), WIDE),
            jax.ShapeDtypeStruct((rows, width), LOW),
            jax.ShapeDtypeStruct((8, width), WIDE),
            jax.ShapeDtypeStruct((1, hidden_width), WIDE),
        ]
        + [jax.ShapeDtypeStruct(shape, LOW) for shape in grads],
        scratch_shapes=[
            pltpu.VMEM((width, width), LOW),
            pltpu.VMEM((width, hidden_width), LOW),
            pltpu.VMEM((hidden_width, width), LOW),
            pltpu.VMEM((rows, hidden_width), LOW),
            pltpu.VMEM((rows, hidden_width), WIDE),
            pltpu.VMEM((rows, width), WIDE),
            pltpu.VMEM((rows, width), LOW),
            pltpu.VMEM((rows, width), LOW),
            pltpu.VMEM((width, hidden_width + width), LOW),
            pltpu.VMEM((hidden_width, width), LOW),
            pltpu.SemaphoreType.DMA((3,)),
            pltpu.SemaphoreType.DMA((8,)),
            pltpu.SemaphoreType.DMA((8,)),
            pltpu.SemaphoreType.DMA((8,)),
        ],
        compiler_params=pltpu.CompilerParams(vmem_limit_bytes=58 << 20),
        cost_estimate=pl.CostEstimate(
            flops=16 * rows * width * hidden_width,
            transcendentals=rows * hidden_width,
            bytes_accessed=12 * width * hidden_width,
        ),
        name="ffn_stage",
    )(places, first, cross, cotangent, vectors, hidden_bias, early, ffn_in, ffn_out)


def apart(start, width):
    pair, half = divmod(start // PAIR, 2)
    return half * width + pair * PAIR


def slotted_products(places, groups, extra=()):
    arrays = [value for group in groups for pair in group for value in pair]
    width = arrays[0].shape[1]
    widths = [group[0][1].shape[1] for group in groups]
    columns = sum(widths) + (128 if extra else 0)
    extras = [part[0] for part in extra]

    def kernel(place_ref, *refs):
        inputs, refs = refs[: len(arrays)], refs[len(arrays) :]
        extra_refs, refs = refs[: len(extras)], refs[len(extras) :]
        keep_ref, send_ref = refs[:2]
        buffers, (rows_ref, total, load_sem, store_sem) = refs[2:-4], refs[-4:]
        loads = [
            pltpu.make_async_copy(inputs[number], buffers[number], load_sem.at[number])
            for number in range(len(arrays))
        ]
        for load in loads:
            load.start()
        copies = []

        def leave(number, at, size):
            group = slot_copies(
                total, keep_ref, send_ref, place_ref, store_sem.at[number], pl.ds(at, size)
            )
            for copy in group:
                copy.start()
            copies.extend(group)

        at = number = 0
        for index, group in enumerate(groups):
            value = None
            for _ in group:
                loads[number].wait()
                loads[number + 1].wait()
                term = left_transposed(buffers[number][...], buffers[number + 1][...])
                value = term if value is None else value + term
                number += 2
            value = value.astype(LOW)
            for start in range(0, widths[index], PAIR):
                given = at + (start if widths[index] == width else apart(start, width))
                total[:, given : given + PAIR] = value[:, start : start + PAIR]
            leave(index, at, widths[index])
            at += widths[index]
        if extras:
            rows_ref[...] = jnp.zeros_like(rows_ref)
            for extra_ref, (_, first, given, count) in zip(extra_refs, extra):
                rows_ref[given : given + count] = extra_ref[first : first + count]
            total[:, at:] = jnp.transpose(rows_ref[...]).astype(LOW)
            leave(len(groups), at, columns - at)
        for copy in copies:
            copy.wait()

    outside = pl.BlockSpec(memory_space=pl.ANY)
    shape = jax.ShapeDtypeStruct((4, width // 8, columns), LOW)
    return pl.pallas_call(
        kernel,
        in_specs=[pl.BlockSpec(memory_space=pltpu.SMEM)]
        + [outside] * len(arrays)
        + [pl.BlockSpec(memory_space=pltpu.VMEM)] * len(extras),
        out_specs=[outside] * 2,
        out_shape=[shape] * 2,
        scratch_shapes=[pltpu.VMEM(value.shape, LOW) for value in arrays]
        + [
            pltpu.VMEM((128, width), WIDE),
            pltpu.VMEM((width, columns), LOW),
            pltpu.SemaphoreType.DMA((len(arrays),)),
            pltpu.SemaphoreType.DMA((len(groups) + 1, 8)),
        ],
        compiler_params=pltpu.CompilerParams(vmem_limit_bytes=58 << 20),
        cost_estimate=pl.CostEstimate(
            flops=2 * width * sum(left.size // width * right.shape[1]
                                  for group in groups for left, right in group),
            transcendentals=0,
            bytes_accessed=sum(2 * value.size for value in arrays) + 2 * width * columns,
        ),
        name="slotted_products",
    )(places, *arrays, *extras)


def plain_products(groups):
    found = [sum([left_transposed(*pair) for pair in group]) for group in groups]
    width = found[0].shape[1]
    found = [part if part.shape[1] == width else deinterleaved(part) for part in found]
    return jnp.concatenate([part.astype(LOW) for part in found], axis=1)


def gathered_back(own, groups):
    slots = [own]
    around = lax.ppermute(own, "seq", [(source, (source - 1) % groups) for source in range(groups)])
    for step in range(1, groups - 1):
        pairs = [(source, source + 1) for source in range(step - 1, groups - 1)]
        slots.append(lax.ppermute(slots[-1], "seq", pairs))
    return slots + [around]


def scatter_steps(slots, groups):
    ring = [(source, (source + 1) % groups) for source in range(groups)]
    if groups == 4:
        parts = [moved(slots[2], "seq", [(3, 2), (2, 1)]), moved(slots[3], "seq", ring)]
        ahead, around = yield parts
        back = [(source, source - 1) for source in range(1, groups)]
        last, around = yield [moved(plus(slots[1], ahead), "seq", back), around]
        parts = [around, last]
    else:
        parts = [moved(slots[groups - 1], "seq", ring)]
        for step in range(groups - 2, 0, -1):
            pairs = [(source, source - step) for source in range(step, groups)]
            parts.append(moved(slots[step], "seq", pairs))
        parts = yield parts
    return sum([part.astype(WIDE) for part in parts], slots[0].astype(WIDE))


class Order:
    token = None

    def hold(self, value):
        if self.token is not None:
            self.token, value = lax.optimization_barrier((self.token, value))
        return value


timeline = Order()


def moved(value, axis_name, pairs):
    return lax.ppermute(timeline.hold(value), axis_name, pairs)


def tied(value, *others):
    return lax.optimization_barrier((value,) + others)[0]


def by_bit(bit, own, other, axis=0):
    own, other = jnp.expand_dims(own, axis), jnp.expand_dims(other, axis)
    return jnp.where(
        bit == 0,
        jnp.concatenate([own, other], axis=axis),
        jnp.concatenate([other, own], axis=axis),
    )


def crossed(value, axis_name, masks):
    count = lax.axis_size(axis_name)
    pairs = [(source, source ^ masks[source % len(masks)]) for source in range(count)]
    return moved(value, axis_name, pairs)


CORE = (1,)
FIRST = (2, 4)
SECOND = (4, 2)


def chip_masks(core):
    first = jnp.where(core == 0, 1, 2)
    return first, 3 - first


def gather_rows(shard):
    return lax.all_gather(shard, "dp", axis=0, tiled=True)


def picked(values, position, axis=0):
    return lax.dynamic_index_in_dim(values, position, axis, keepdims=False)


def plus(left, right):
    return (left.astype(WIDE) + right.astype(WIDE)).astype(LOW)


def summed(*parts):
    return sum([part.astype(WIDE) for part in parts]).astype(LOW)


class Chain:
    def __init__(self, steps):
        self.steps = steps
        self.pending = next(steps)
        self.result = None

    def step(self):
        if self.result is None:
            try:
                self.pending = self.steps.send(self.pending)
            except StopIteration as stop:
                self.result = stop.value

    def advance(self):
        if self.result is None:
            self.pending = timeline.hold(self.pending)
            self.step()


def pumped(values, *chains):
    live = [chain for chain in chains if chain.result is None]
    values, arrived = lax.optimization_barrier((values, [chain.pending for chain in live]))
    for chain, brought in zip(live, arrived):
        chain.pending = brought
        chain.step()
    return values


def finished(*chains, ahead=()):
    for chain in ahead:
        chain.advance()
    while any(chain.result is None for chain in chains):
        for chain in chains:
            chain.advance()
    return [chain.result for chain in chains]


def places_steps(sums):
    place = lax.axis_index("seq")
    sums = plus(sums, (yield moved(sums, "seq", [(0, 1), (3, 2)])))
    sums = plus(sums, (yield moved(sums, "seq", [(1, 2), (2, 1)])))
    back = yield moved(sums, "seq", [(1, 0), (2, 3)])
    return jnp.where((place == 0) | (place == 3), back, sums)


def offloaded_steps(gradient):
    share = yield lax.psum_scatter(gradient, "dp", scatter_dimension=0, tiled=True)
    if lax.axis_size("dp") != 8 or lax.axis_size("seq") != 4:
        return (yield lax.psum(share, "seq")).astype(WIDE)
    return (yield from places_steps(share)).astype(WIDE)


def slot_steps(keep, send):
    core = yield crossed(send, "dp", CORE)
    one = yield crossed(summed(keep[2:], core[2:]), "dp", FIRST)
    two = yield crossed(summed(keep[1], core[1], one[1]), "dp", SECOND)
    share = summed(keep[0], core[0], one[0], two)
    return (yield from places_steps(share)).astype(WIDE)


def slot_places():
    index = lax.axis_index("dp")
    core, chip = index % 2, index // 2

    def slots(core):
        first, second = chip_masks(core)
        away = jnp.arange(4) ^ chip
        return jnp.where(away == 0, 0, jnp.where(away == second, 1, jnp.where(away == first, 2, 3)))

    places = jnp.concatenate([core[None], slots(core), slots(1 - core)])
    return places.astype(jnp.int32)


def gather_small(values):
    if lax.axis_size("dp") != 8:
        return lax.all_gather(values, "dp", axis=0)
    index = lax.axis_index("dp")
    out = by_bit(index % 2, values, crossed(values, "dp", CORE))
    out = by_bit(index // 2 % 2, out, crossed(out, "dp", (2,)))
    out = by_bit(index // 4, out, crossed(out, "dp", (4,)))
    return out.reshape((8,) + values.shape)


def small_steps(values):
    if lax.axis_size("dp") != 8 or lax.axis_size("seq") != 4:
        return (yield lax.psum(values, ("dp", "seq")))
    for axis_name, mask in (("dp", 1), ("dp", 2), ("dp", 4), ("seq", 1), ("seq", 2)):
        values = values + (yield crossed(values, axis_name, (mask,)))
    return values


def gather_steps(values):
    if lax.axis_size("seq") != 4:
        return (yield lax.all_gather(values, "seq", axis=0))
    place = lax.axis_index("seq")
    out = by_bit(place % 2, values, (yield crossed(values, "seq", (1,))))
    out = by_bit(place // 2, out, (yield crossed(out, "seq", (2,))))
    return out.reshape((4,) + values.shape)


def chunk_steps(values):
    if lax.axis_size("seq") != 4:
        return (yield lax.psum_scatter(values, "seq", scatter_dimension=0, tiled=False)).astype(WIDE)
    place = lax.axis_index("seq")
    low_bit, high_bit = place % 2, place // 2
    values = values.reshape((2, 2) + values.shape[1:])
    going = picked(values, 1 - low_bit, 1)
    values = plus(picked(values, low_bit, 1), (yield crossed(going, "seq", (1,))))
    going = picked(values, 1 - high_bit)
    return picked(values, high_bit).astype(WIDE) + (yield crossed(going, "seq", (2,))).astype(WIDE)


def interleaved(keys_values):
    rows, columns = keys_values.shape
    view = keys_values.reshape(rows, 2, columns // (2 * PAIR), PAIR)
    return view.transpose(0, 2, 1, 3).reshape(rows, columns)


def deinterleaved(keys_values):
    rows, columns = keys_values.shape
    view = keys_values.reshape(rows, columns // (2 * PAIR), 2, PAIR)
    return view.transpose(0, 2, 1, 3).reshape(rows, columns)


def local(
    tokens,
    encoded,
    cotangent,
    attn_in,
    attn_out,
    cross_in,
    cross_out,
    ffn_in,
    ffn_out,
    gains,
    biases,
    bias_ff,
    block_ids,
    enc_lengths,
):
    groups = lax.axis_size("seq")
    shards = lax.axis_size("dp")
    place = lax.axis_index("seq")
    owner = lax.axis_index("dp")
    batch, local_len, width = tokens.shape
    enc_local = encoded.shape[1]
    rows = batch * local_len
    length = local_len * groups
    enc_length = enc_local * groups
    hidden_width = ffn_in.shape[1]
    slotted = shards == 8 and groups == 4
    places = slot_places() if slotted else jnp.zeros((9,), jnp.int32)

    attn_q, attn_kv = attn_in[:, :width], interleaved(attn_in[:, width:])
    cross_q, cross_kv = cross_in[:, :width], interleaved(cross_in[:, width:])
    early = gather_rows(
        jnp.concatenate([attn_q, attn_kv, attn_out, cross_q, cross_kv, cross_out], axis=1)
    )
    slots = gathered_back(tokens, groups)
    small = jnp.concatenate([gains, biases, bias_ff.reshape(-1, gains.shape[1])], axis=0)
    small = gather_small(small)
    small = small.astype(WIDE)
    gain_rows = gains.shape[0]
    bias_rows = biases.shape[0]
    vectors = small[:, : gain_rows + bias_rows].transpose(1, 0, 2).reshape(-1, width)
    gain_all = vectors[:gain_rows]
    bias_all = vectors[gain_rows:]
    bias_hidden = small[:, gain_rows + bias_rows :].reshape(hidden_width)
    blank = jnp.zeros((width,), WIDE)
    value_bias = interleaved(jnp.concatenate([blank, bias_all[1]])[None])
    cross_value_bias = interleaved(jnp.concatenate([blank, bias_all[4]])[None])

    chunks = block_ids.reshape(batch, groups, local_len)
    order = (place - jnp.arange(groups)) % groups
    kid = jnp.take(chunks, order, axis=1).reshape(batch, length)
    qid = kid[:, :local_len]
    enc_kid = jnp.broadcast_to(jnp.arange(enc_length, dtype=jnp.int32)[None], (batch, enc_length))
    enc_qid = jnp.broadcast_to(enc_lengths[:, None] - 1, (batch, local_len))
    ids = (kid[:, None, :], kid[:, :, None], qid[:, None, :], qid[:, :, None])
    enc_ids = (enc_kid[:, None, :], enc_kid[:, :, None], enc_qid[:, None, :], enc_qid[:, :, None])

    vectors = (gain_all, bias_all, bias_hidden, value_bias, cross_value_bias)
    early, slots, vectors, ids, enc_ids = lax.optimization_barrier(
        (early, slots, vectors, ids, enc_ids)
    )
    gain_all, bias_all, bias_hidden, value_bias, cross_value_bias = vectors
    attn_q, attn_kv = early[:, :width], early[:, width : 3 * width]
    attn_out, cross_q = early[:, 3 * width : 4 * width], early[:, 4 * width : 5 * width]
    cross_kv = early[:, 5 * width : 7 * width]
    ffn_in = gather_rows(ffn_in)
    ffn_out = gather_rows(ffn_out)
    enc_gather = Chain(gather_steps(tied(encoded, slots[-1])))

    token_each = [
        jnp.concatenate([slot[number] for slot in slots], axis=0) for number in range(batch)
    ]
    token_flat = tokens.reshape(rows, width)
    queries = (product(token_flat, attn_q) + bias_all[0]).astype(LOW)
    queries = queries.reshape(batch, local_len, width)
    keys_values = jnp.stack(
        [(product(each, attn_kv) + value_bias).astype(LOW) for each in token_each]
    )

    queries, keys_values = pumped((queries, keys_values), enc_gather)
    context, totals = attend_forward(queries, keys_values, ids)
    context = pumped(context, enc_gather)
    encoded = enc_gather.result
    enc_all = encoded.transpose(1, 0, 2, 3).reshape(batch * enc_length, width)
    enc_kv = (product(enc_all, cross_kv) + cross_value_bias).astype(LOW)
    enc_kv = enc_kv.reshape(batch, enc_length, 2 * width)
    context_flat = context.reshape(rows, width)
    first_sum = token_flat.astype(WIDE) + product(context_flat, attn_out) + bias_all[2]
    first = layer_norm(first_sum, gain_all[0], bias_all[7])
    first_low = first.astype(LOW)
    cross_queries = (product(first_low, cross_q) + bias_all[3]).astype(LOW)
    cross_queries = cross_queries.reshape(batch, local_len, width)
    cross_context, cross_totals = attend_forward(cross_queries, enc_kv, enc_ids)
    cross_flat = cross_context.reshape(rows, width)
    stage_vectors = jnp.stack(
        [bias_all[5], gain_all[1], bias_all[8], bias_all[6], gain_all[2], bias_all[9]]
    )
    final, d_second_sum, d_cross_ctx, sums, d_bias_hidden, *grads = ffn_stage(
        places,
        first,
        cross_flat,
        cotangent.reshape(rows, width),
        stage_vectors,
        bias_hidden[None],
        early,
        ffn_in,
        ffn_out,
        slotted,
    )
    if slotted:
        out_chain = Chain(slot_steps(*grads[2:]))
        in_chain = Chain(slot_steps(*grads[:2]))
    else:
        out_chain = Chain(offloaded_steps(grads[1]))
        in_chain = Chain(offloaded_steps(grads[0]))

    def gradient_chain(groups, after, extra=()):
        if slotted:
            products = slotted_products(places, groups, extra)
            products, after = lax.optimization_barrier((products, after))
            return Chain(slot_steps(*products)), after
        gradient, after = lax.optimization_barrier((plain_products(groups), after))
        return Chain(offloaded_steps(gradient)), after

    d_cross_ctx = d_cross_ctx.reshape(cross_context.shape)
    d_cross_q, d_enc = attend_backward(
        cross_queries, enc_kv, enc_ids, cross_context, d_cross_ctx, cross_totals, 0, batch
    )
    d_cross_q, d_enc = pumped((d_cross_q, d_enc), out_chain, in_chain)
    d_cross_q = d_cross_q.reshape(rows, width)
    d_enc = d_enc.reshape(-1, 2 * width)
    d_encoded = right_transposed(d_enc, cross_kv)
    d_encoded = d_encoded.reshape(batch, groups, enc_local, width).astype(LOW)
    d_encoded, d_cross_q = lax.optimization_barrier((d_encoded, d_cross_q))
    enc_chain = Chain(chunk_steps(d_encoded.transpose(1, 0, 2, 3)))
    d_first = d_second_sum + right_transposed(d_cross_q, cross_q)
    d_first_sum, d_gain_one, d_offset_one = norm_backward(first_sum, gain_all[0], d_first)
    d_attn = d_first_sum.astype(LOW)
    d_context = right_transposed(d_attn, attn_out).astype(LOW).reshape(context.shape)
    d_context = pumped(d_context, out_chain, enc_chain)
    left = (context_flat, first_low, enc_all, d_attn, d_cross_q, d_enc)
    left, d_context = lax.optimization_barrier((left, d_context))
    mid_chain, d_context = gradient_chain([[pair] for pair in zip(left[:3], left[3:])], d_context)

    def token_chain(d_kv, after):
        d_part = right_transposed(d_kv, attn_kv).astype(LOW)
        d_part, after = lax.optimization_barrier((d_part, after))
        d_part = d_part.reshape(groups, local_len, width)
        return Chain(scatter_steps(list(d_part), groups)), after

    d_query, d_key_value, token_chains = [], [], []
    for number in range(batch):
        d_q, d_kv = attend_backward(
            queries, keys_values, ids, context, d_context, totals, number, 1
        )
        pumps = (out_chain, in_chain, mid_chain, enc_chain)[: 2 if number else 4]
        d_q, d_kv, d_context = pumped((d_q[0], d_kv[0], d_context), *pumps)
        d_query.append(d_q)
        if number == 0:
            chain, (d_kv, d_context) = token_chain(d_kv, (d_kv, d_context))
            token_chains.append(chain)
        d_key_value.append(d_kv)
    part = width // shards
    hidden_rows = d_bias_hidden.reshape(shards, -1, part).transpose(1, 0, 2).reshape(-1, width)
    vectors = gain_rows + bias_rows + hidden_rows.shape[0]
    query_rows = column_total(jnp.concatenate(d_query, axis=0))[None]
    singles = [d_gain_one[None], query_rows]
    singles += [column_total(d_context.reshape(rows, width))[None], column_total(d_attn)[None]]
    singles += [column_total(d_cross_q)[None], d_offset_one[None]]
    extra = [(one, 0, at, 1) for one, at in zip(singles, (0, 3, 4, 5, 6, 10))]
    extra += [(sums, row, at, 1) for row, at in enumerate((2, 12, 9, 1, 11, 8, 7))]
    extra.append((hidden_rows, 0, gain_rows + bias_rows, hidden_rows.shape[0]))
    query_rows = jnp.concatenate(d_query, axis=0)
    query_rows, d_query, d_key_value = lax.optimization_barrier((query_rows, d_query, d_key_value))
    attn_chain, (query_rows, d_key_value) = gradient_chain(
        [
            list(zip([tokens[number] for number in range(batch)], d_query)),
            list(zip(token_each, d_key_value)),
        ],
        (query_rows, d_key_value),
        extra,
    )
    query_rows, d_key_value = pumped(
        (query_rows, d_key_value), mid_chain, out_chain, token_chains[0]
    )
    for d_kv in d_key_value[1:]:
        chain, query_rows = token_chain(d_kv, query_rows)
        token_chains.append(chain)
    query_rows = pumped(query_rows, attn_chain, in_chain)
    d_tokens = d_first_sum + right_transposed(query_rows, attn_q)
    timeline.token = d_tokens.reshape(tokens.shape)
    early, late = token_chains[0], token_chains[-1]
    early, late = token_chains[0], token_chains[-1]
    ahead = [mid_chain, out_chain, attn_chain, early, in_chain, mid_chain, attn_chain, late]
    ahead += [in_chain, mid_chain, attn_chain, mid_chain, attn_chain, late]
    chains = [attn_chain, mid_chain, in_chain, out_chain, enc_chain]
    grad_attn, middle, grad_in, grad_ffn_out, d_encoded, *d_parts = finished(
        *chains, *token_chains, ahead=ahead
    )
    d_tokens, timeline.token = timeline.token, None
    d_tokens = d_tokens + jnp.stack(d_parts)
    if slotted:
        mine = grad_attn[:, 3 * width :].T
    else:
        vector_grads = jnp.zeros((vectors, width), WIDE)
        for value, first, at, count in extra:
            vector_grads = vector_grads.at[at : at + count].set(value[first : first + count])
        (vector_grads,) = finished(Chain(small_steps(vector_grads)))
        mine = lax.dynamic_slice_in_dim(vector_grads, owner * part, part, axis=1)
    grad_cross_out = grad_in[:, hidden_width:]
    return (
        final.reshape(batch, local_len, width),
        d_tokens,
        d_encoded,
        grad_attn[:, : 3 * width],
        middle[:, :width],
        middle[:, width : 4 * width],
        grad_cross_out,
        grad_in[:, :hidden_width],
        grad_ffn_out,
        mine[:gain_rows],
        mine[gain_rows : gain_rows + bias_rows],
        mine[gain_rows + bias_rows : vectors].reshape(-1),
    )


def solution(mesh):
    split = P("dp", "seq", None)
    rows = P("dp", None)
    columns = P(None, "dp")
    vector = P("dp")
    in_specs = (split,) * 3 + (rows,) * 6 + (columns, columns, vector, rows, vector)
    out_specs = (split,) * 3 + (rows,) * 6 + (columns, columns, vector)
    return jax.shard_map(local, mesh=mesh, in_specs=in_specs, out_specs=out_specs, check_vma=False)
```

```python
import jax
import jax.numpy as jnp
from jax import lax
from jax.experimental import pallas as pl
from jax.experimental.pallas import tpu as pltpu
from jax.sharding import PartitionSpec as P

HD = 64
PAIR = 2 * HD
EPSILON = 1e-05
MASKED = -1e30
LOW = jnp.bfloat16
WIDE = jnp.float32


def product(left, right):
    return jnp.dot(left, right, preferred_element_type=WIDE)


def left_transposed(left, right):
    return lax.dot_general(left, right, (((0,), (0,)), ((), ())), preferred_element_type=WIDE)


def right_transposed(left, right):
    return lax.dot_general(left, right, (((1,), (1,)), ((), ())), preferred_element_type=WIDE)


def column_total(values):
    return jnp.sum(values.astype(WIDE), axis=0)


def layer_norm(summed, gain, offset):
    centre = summed - jnp.mean(summed, axis=-1, keepdims=True)
    spread = jnp.mean(centre * centre, axis=-1, keepdims=True)
    return centre * lax.rsqrt(spread + EPSILON) * gain + offset


def norm_backward(summed, gain, upstream):
    centre = summed - jnp.mean(summed, axis=-1, keepdims=True)
    spread = jnp.mean(centre * centre, axis=-1, keepdims=True)
    inverse = lax.rsqrt(spread + EPSILON)
    unit = centre * inverse
    scaled = upstream * gain
    mean_scaled = jnp.mean(scaled, axis=-1, keepdims=True)
    mean_both = jnp.mean(scaled * unit, axis=-1, keepdims=True)
    d_summed = (scaled - mean_scaled - unit * mean_both) * inverse
    return d_summed, jnp.sum(upstream * unit, axis=0), jnp.sum(upstream, axis=0)


def stacked_heads(values):
    lane = lax.broadcasted_iota(jnp.int32, values.shape, 1)
    none = jnp.zeros_like(values)
    return jnp.concatenate(
        [jnp.where(lane < HD, values, none), jnp.where(lane >= HD, values, none)], axis=0
    )


def merged_heads(stacked):
    half = stacked.shape[0] // 2
    lane = lax.broadcasted_iota(jnp.int32, (half, PAIR), 1)
    return jnp.where(lane < HD, stacked[:half], stacked[half:])


def forward_kernel(q_ref, kv_ref, qid_ref, kid_ref, o_ref, total_ref):
    queries = stacked_heads(q_ref[0]) * jnp.asarray(HD**-0.5, LOW)
    scores = right_transposed(queries, kv_ref[0, :, :PAIR])
    qid = qid_ref[0]
    allowed = kid_ref[0] <= jnp.concatenate([qid, qid], axis=0)
    scores = jnp.where(allowed, scores, MASKED)
    highest = jnp.max(scores, axis=-1, keepdims=True)
    exponent = jnp.exp(scores - highest)
    denominator = jnp.sum(exponent, axis=-1, keepdims=True)
    context = product(exponent.astype(LOW), kv_ref[0, :, PAIR:]) / denominator
    o_ref[0] = merged_heads(context).astype(LOW)
    totals = highest + jnp.log(denominator)
    total_ref[0, 0] = jnp.transpose(jnp.broadcast_to(totals, (totals.shape[0], 128)))[:8]


def backward_kernel(q_ref, kv_ref, qid_ref, kid_ref, o_ref, do_ref, total_ref, dq_ref, dkv_ref):
    queries = stacked_heads(q_ref[0]) * jnp.asarray(HD**-0.5, LOW)
    upstream = stacked_heads(do_ref[0])
    both = do_ref[0].astype(WIDE) * o_ref[0].astype(WIDE)
    row = lax.broadcasted_iota(jnp.int32, (8, PAIR), 0)
    lane = lax.broadcasted_iota(jnp.int32, (8, PAIR), 1)
    pick = jnp.where(lane // HD == row, 1.0, 0.0).astype(WIDE)
    inner = lax.dot_general(
        pick,
        both,
        (((1,), (1,)), ((), ())),
        precision=lax.Precision.HIGHEST,
        preferred_element_type=WIDE,
    )
    inner = jnp.concatenate([inner[0:1], inner[1:2]], axis=1)
    keys = kv_ref[0, :, :PAIR]
    qid = qid_ref[0]
    allowed = kid_ref[0] <= jnp.concatenate([qid, qid], axis=1)
    scores = jnp.where(allowed, right_transposed(keys, queries), MASKED)
    weights = jnp.exp(scores - total_ref[0, 0, 0:1])
    dkv_ref[0, :, PAIR:] = product(weights.astype(LOW), upstream).astype(LOW)
    weight_grads = right_transposed(kv_ref[0, :, PAIR:], upstream)
    score_grads = (weights * (weight_grads - inner)).astype(LOW)
    dkv_ref[0, :, :PAIR] = product(score_grads, queries).astype(LOW)
    dq = left_transposed(score_grads, keys) * (HD**-0.5)
    dq_ref[0] = merged_heads(dq).astype(LOW)


def attend_forward(queries, keys_values, ids):
    batch, rows, width = queries.shape
    keys = keys_values.shape[1]
    pairs = width // PAIR
    one = pl.BlockSpec((1, rows, PAIR), lambda b, p: (b, 0, p))
    work = batch * pairs * rows * keys
    return pl.pallas_call(
        forward_kernel,
        grid=(batch, pairs),
        in_specs=[
            one,
            pl.BlockSpec((1, keys, 2 * PAIR), lambda b, p: (b, 0, p)),
            pl.BlockSpec((1, rows, 1), lambda b, p: (b, 0, 0)),
            pl.BlockSpec((1, 1, keys), lambda b, p: (b, 0, 0)),
        ],
        out_specs=[one, pl.BlockSpec((1, 1, 8, 2 * rows), lambda b, p: (b, p, 0, 0))],
        out_shape=[
            jax.ShapeDtypeStruct((batch, rows, width), LOW),
            jax.ShapeDtypeStruct((batch, pairs, 8, 2 * rows), WIDE),
        ],
        cost_estimate=pl.CostEstimate(
            flops=4000 * work, transcendentals=2 * work, bytes_accessed=8 * batch * keys * width
        ),
        name="attend_forward",
    )(queries, keys_values, ids[3], ids[0])


def attend_backward(queries, keys_values, ids, context, upstream, totals, start, count):
    _, rows, width = queries.shape
    keys = keys_values.shape[1]
    pairs = width // PAIR
    one = pl.BlockSpec((1, rows, PAIR), lambda b, p: (start + b, 0, p))
    work = count * pairs * rows * keys
    return pl.pallas_call(
        backward_kernel,
        grid=(count, pairs),
        in_specs=[
            one,
            pl.BlockSpec((1, keys, 2 * PAIR), lambda b, p: (start + b, 0, p)),
            pl.BlockSpec((1, 1, rows), lambda b, p: (start + b, 0, 0)),
            pl.BlockSpec((1, keys, 1), lambda b, p: (start + b, 0, 0)),
            one,
            one,
            pl.BlockSpec((1, 1, 8, 2 * rows), lambda b, p: (start + b, p, 0, 0)),
        ],
        out_specs=[
            pl.BlockSpec((1, rows, PAIR), lambda b, p: (b, 0, p)),
            pl.BlockSpec((1, keys, 2 * PAIR), lambda b, p: (b, 0, p)),
        ],
        out_shape=[
            jax.ShapeDtypeStruct((count, rows, width), LOW),
            jax.ShapeDtypeStruct((count, keys, 2 * width), LOW),
        ],
        cost_estimate=pl.CostEstimate(
            flops=4000 * work, transcendentals=2 * work, bytes_accessed=8 * count * keys * width
        ),
        name="attend_backward",
    )(queries, keys_values, ids[2], ids[1], context, upstream, totals)


CHUNK = 768


def normalised(summed):
    centre = summed - jnp.mean(summed, axis=-1, keepdims=True)
    inverse = lax.rsqrt(jnp.mean(centre * centre, axis=-1, keepdims=True) + EPSILON)
    return centre * inverse, inverse


def normalised_backward(unit, inverse, scaled):
    mean_scaled = jnp.mean(scaled, axis=-1, keepdims=True)
    mean_both = jnp.mean(scaled * unit, axis=-1, keepdims=True)
    return (scaled - mean_scaled - unit * mean_both) * inverse


def gelu_pair(values):
    size = jnp.abs(values) * (0.5**0.5)
    bell = jnp.exp(-0.5 * values * values)
    t = 1.0 / (1.0 + 0.3275911 * size)
    series = t * (
        0.127414796
        + t * (-0.142248368 + t * (0.7107068705 + t * (-0.7265760135 + t * 0.5307027145)))
    )
    tail = series * bell
    below = jnp.where(values >= 0, 1.0 - tail, tail)
    return values * below, below + values * bell * 0.3989422804014327


def total_row(values):
    return jnp.sum(values, axis=0, keepdims=True)


def slot_copies(source, keep_ref, send_ref, place_ref, semaphores, columns=None, chips=None):
    rows = keep_ref.shape[1]
    core = place_ref[0]
    found = []
    for chip in range(4) if chips is None else chips:
        for number, (slots_ref, owner) in enumerate(((keep_ref, core), (send_ref, 1 - core))):
            at = pl.ds(pl.multiple_of((2 * chip + owner) * rows, 16), rows)
            slot = place_ref[1 + 4 * number + chip]
            taken, given = source.at[at], slots_ref.at[slot]
            if columns is not None:
                taken, given = source.at[at, columns], slots_ref.at[slot, :, columns]
            found.append(pltpu.make_async_copy(taken, given, semaphores.at[2 * chip + number]))
    return found


def ffn_kernel(
    place_ref,
    first_ref,
    cross_ref,
    cot_ref,
    vector_ref,
    hidden_bias_ref,
    early_ref,
    in_ref,
    out_ref,
    final_ref,
    d_sum_ref,
    d_ctx_ref,
    sums_ref,
    hidden_sums_ref,
    *others,
):
    grad_refs, scratch = others[:-14], others[-14:]
    w_cross, w_in, w_out, hidden, slope, total, low, d_low, g_in, g_out = scratch[:10]
    load_sem, out_sem, in_sem, cross_sem = scratch[10:14]
    rows, width = first_ref.shape
    hidden_width = w_in.shape[1]
    count = hidden_width // CHUNK
    slotted = len(grad_refs) == 4
    cross_at = early_ref.shape[1] - width
    loads = [
        pltpu.make_async_copy(early_ref.at[:, cross_at:], w_cross, load_sem.at[0]),
        pltpu.make_async_copy(in_ref, w_in, load_sem.at[1]),
        pltpu.make_async_copy(out_ref, w_out, load_sem.at[2]),
    ]
    for load in loads:
        load.start()
    loads[0].wait()
    second_sum = first_ref[...] + product(cross_ref[...], w_cross[...]) + vector_ref[0:1]
    unit, inverse = normalised(second_sum)
    second = unit * vector_ref[1:2] + vector_ref[2:3]
    low[...] = second.astype(LOW)
    total[...] = second + vector_ref[3:4]
    d_sum_ref[...] = unit
    loads[1].wait()
    loads[2].wait()

    def forward(step, carry):
        at = pl.ds(pl.multiple_of(step * CHUNK, CHUNK), CHUNK)
        activation = product(low[...], w_in[:, at]) + hidden_bias_ref[:, at]
        value, slope_value = gelu_pair(activation)
        value = value.astype(LOW)
        hidden[:, at] = value
        slope[:, at] = slope_value
        total[...] += product(value, w_out[at, :])
        return carry

    lax.fori_loop(0, count, forward, 0)
    third, third_inverse = normalised(total[...])
    final_ref[...] = (third * vector_ref[4:5] + vector_ref[5:6]).astype(LOW)
    upstream = cot_ref[...].astype(WIDE)
    sums_ref[0:1] = total_row(upstream * third)
    sums_ref[1:2] = total_row(upstream)
    d_third = normalised_backward(third, third_inverse, upstream * vector_ref[4:5])
    d_low[...] = d_third.astype(LOW)
    sums_ref[2:3] = total_row(d_low[...].astype(WIDE))
    total[...] = d_third

    def backward(step, carry):
        at = pl.ds(pl.multiple_of(step * CHUNK, CHUNK), CHUNK)
        g_out[at, :] = left_transposed(hidden[:, at], d_low[...]).astype(LOW)
        d_hidden = right_transposed(d_low[...], w_out[at, :])
        d_activation = (d_hidden * slope[:, at]).astype(LOW)
        hidden_sums_ref[:, at] = total_row(d_activation.astype(WIDE))
        g_in[:, at] = left_transposed(low[...], d_activation).astype(LOW)
        total[...] += right_transposed(d_activation, w_in[:, at])
        if slotted:
            for copy in slot_copies(g_out, *grad_refs[2:], place_ref, out_sem, None, [step]):
                copy.start()
        return carry

    lax.fori_loop(0, count, backward, 0)
    if slotted:
        copies = [
            slot_copies(g_out, *grad_refs[2:], place_ref, out_sem),
            slot_copies(
                g_in, *grad_refs[:2], place_ref, in_sem, pl.ds(0, hidden_width)
            ),
            slot_copies(
                g_in, *grad_refs[:2], place_ref, cross_sem, pl.ds(hidden_width, width)
            ),
        ]
    else:
        copies = [
            [pltpu.make_async_copy(g_out, grad_refs[1], out_sem.at[0])],
            [pltpu.make_async_copy(g_in, grad_refs[0], in_sem.at[0])],
        ]
        copies[0][0].start()
    if slotted:
        for copy in copies[1]:
            copy.start()
    d_second = total[...]
    unit = d_sum_ref[...]
    sums_ref[3:4] = total_row(d_second * unit)
    sums_ref[4:5] = total_row(d_second)
    d_second_sum = normalised_backward(unit, inverse, d_second * vector_ref[1:2])
    d_sum_ref[...] = d_second_sum
    d_cross = d_second_sum.astype(LOW)
    sums_ref[5:6] = total_row(d_cross.astype(WIDE))
    g_in[:, hidden_width:] = left_transposed(cross_ref[...], d_cross).astype(LOW)
    for copy in copies[-1]:
        copy.start()
    d_ctx = right_transposed(d_cross, w_cross[...]).astype(LOW)
    d_ctx_ref[...] = d_ctx
    sums_ref[6:7] = total_row(d_ctx.astype(WIDE))
    sums_ref[7:8] = jnp.zeros_like(sums_ref[7:8])
    for group in copies:
        for copy in group:
            copy.wait()


def ffn_stage(
    places, first, cross, cotangent, vectors, hidden_bias, early, ffn_in, ffn_out, slotted
):
    rows, width = first.shape
    hidden_width = ffn_in.shape[1]
    count = hidden_width // CHUNK
    inside = pl.BlockSpec(memory_space=pltpu.VMEM)
    outside = pl.BlockSpec(memory_space=pl.ANY)
    grads = [(width, hidden_width + width), (hidden_width, width)]
    if slotted:
        grads = [(4, shape[0] // 8, shape[1]) for shape in grads for _ in range(2)]
    return pl.pallas_call(
        ffn_kernel,
        in_specs=[pl.BlockSpec(memory_space=pltpu.SMEM)] + [inside] * 5 + [outside] * 3,
        out_specs=[inside] * 5 + [outside] * len(grads),
        out_shape=[
            jax.ShapeDtypeStruct((rows, width), LOW),
            jax.ShapeDtypeStruct((rows, width), WIDE),
            jax.ShapeDtypeStruct((rows, width), LOW),
            jax.ShapeDtypeStruct((8, width), WIDE),
            jax.ShapeDtypeStruct((1, hidden_width), WIDE),
        ]
        + [jax.ShapeDtypeStruct(shape, LOW) for shape in grads],
        scratch_shapes=[
            pltpu.VMEM((width, width), LOW),
            pltpu.VMEM((width, hidden_width), LOW),
            pltpu.VMEM((hidden_width, width), LOW),
            pltpu.VMEM((rows, hidden_width), LOW),
            pltpu.VMEM((rows, hidden_width), WIDE),
            pltpu.VMEM((rows, width), WIDE),
            pltpu.VMEM((rows, width), LOW),
            pltpu.VMEM((rows, width), LOW),
            pltpu.VMEM((width, hidden_width + width), LOW),
            pltpu.VMEM((hidden_width, width), LOW),
            pltpu.SemaphoreType.DMA((3,)),
            pltpu.SemaphoreType.DMA((8,)),
            pltpu.SemaphoreType.DMA((8,)),
            pltpu.SemaphoreType.DMA((8,)),
        ],
        compiler_params=pltpu.CompilerParams(vmem_limit_bytes=58 << 20),
        cost_estimate=pl.CostEstimate(
            flops=16 * rows * width * hidden_width,
            transcendentals=rows * hidden_width,
            bytes_accessed=12 * width * hidden_width,
        ),
        name="ffn_stage",
    )(places, first, cross, cotangent, vectors, hidden_bias, early, ffn_in, ffn_out)


def apart(start, width):
    pair, half = divmod(start // PAIR, 2)
    return half * width + pair * PAIR


def slotted_products(places, groups, extra=()):
    arrays = [value for group in groups for pair in group for value in pair]
    width = arrays[0].shape[1]
    widths = [group[0][1].shape[1] for group in groups]
    columns = sum(widths) + (128 if extra else 0)
    extras = [part[0] for part in extra]

    def kernel(place_ref, *refs):
        inputs, refs = refs[: len(arrays)], refs[len(arrays) :]
        extra_refs, refs = refs[: len(extras)], refs[len(extras) :]
        keep_ref, send_ref = refs[:2]
        buffers, (rows_ref, total, load_sem, store_sem) = refs[2:-4], refs[-4:]
        loads = [
            pltpu.make_async_copy(inputs[number], buffers[number], load_sem.at[number])
            for number in range(len(arrays))
        ]
        for load in loads:
            load.start()
        copies = []

        def leave(number, at, size):
            group = slot_copies(
                total, keep_ref, send_ref, place_ref, store_sem.at[number], pl.ds(at, size)
            )
            for copy in group:
                copy.start()
            copies.extend(group)

        at = number = 0
        for index, group in enumerate(groups):
            value = None
            for _ in group:
                loads[number].wait()
                loads[number + 1].wait()
                term = left_transposed(buffers[number][...], buffers[number + 1][...])
                value = term if value is None else value + term
                number += 2
            value = value.astype(LOW)
            for start in range(0, widths[index], PAIR):
                given = at + (start if widths[index] == width else apart(start, width))
                total[:, given : given + PAIR] = value[:, start : start + PAIR]
            leave(index, at, widths[index])
            at += widths[index]
        if extras:
            rows_ref[...] = jnp.zeros_like(rows_ref)
            for extra_ref, (_, first, given, count) in zip(extra_refs, extra):
                rows_ref[given : given + count] = extra_ref[first : first + count]
            total[:, at:] = jnp.transpose(rows_ref[...]).astype(LOW)
            leave(len(groups), at, columns - at)
        for copy in copies:
            copy.wait()

    outside = pl.BlockSpec(memory_space=pl.ANY)
    shape = jax.ShapeDtypeStruct((4, width // 8, columns), LOW)
    return pl.pallas_call(
        kernel,
        in_specs=[pl.BlockSpec(memory_space=pltpu.SMEM)]
        + [outside] * len(arrays)
        + [pl.BlockSpec(memory_space=pltpu.VMEM)] * len(extras),
        out_specs=[outside] * 2,
        out_shape=[shape] * 2,
        scratch_shapes=[pltpu.VMEM(value.shape, LOW) for value in arrays]
        + [
            pltpu.VMEM((128, width), WIDE),
            pltpu.VMEM((width, columns), LOW),
            pltpu.SemaphoreType.DMA((len(arrays),)),
            pltpu.SemaphoreType.DMA((len(groups) + 1, 8)),
        ],
        compiler_params=pltpu.CompilerParams(vmem_limit_bytes=58 << 20),
        cost_estimate=pl.CostEstimate(
            flops=2 * width * sum(left.size // width * right.shape[1]
                                  for group in groups for left, right in group),
            transcendentals=0,
            bytes_accessed=sum(2 * value.size for value in arrays) + 2 * width * columns,
        ),
        name="slotted_products",
    )(places, *arrays, *extras)


def plain_products(groups):
    found = [sum([left_transposed(*pair) for pair in group]) for group in groups]
    width = found[0].shape[1]
    found = [part if part.shape[1] == width else deinterleaved(part) for part in found]
    return jnp.concatenate([part.astype(LOW) for part in found], axis=1)


def gathered_back(own, groups):
    slots = [own]
    around = lax.ppermute(own, "seq", [(source, (source - 1) % groups) for source in range(groups)])
    for step in range(1, groups - 1):
        pairs = [(source, source + 1) for source in range(step - 1, groups - 1)]
        slots.append(lax.ppermute(slots[-1], "seq", pairs))
    return slots + [around]


def scatter_steps(slots, groups):
    ring = [(source, (source + 1) % groups) for source in range(groups)]
    if groups == 4:
        parts = [moved(slots[2], "seq", [(3, 2), (2, 1)]), moved(slots[3], "seq", ring)]
        ahead, around = yield parts
        back = [(source, source - 1) for source in range(1, groups)]
        last, around = yield [moved(plus(slots[1], ahead), "seq", back), around]
        parts = [around, last]
    else:
        parts = [moved(slots[groups - 1], "seq", ring)]
        for step in range(groups - 2, 0, -1):
            pairs = [(source, source - step) for source in range(step, groups)]
            parts.append(moved(slots[step], "seq", pairs))
        parts = yield parts
    return sum([part.astype(WIDE) for part in parts], slots[0].astype(WIDE))


class Order:
    token = None

    def hold(self, value):
        if self.token is not None:
            self.token, value = lax.optimization_barrier((self.token, value))
        return value


timeline = Order()


def moved(value, axis_name, pairs):
    return lax.ppermute(timeline.hold(value), axis_name, pairs)


def tied(value, *others):
    return lax.optimization_barrier((value,) + others)[0]


def by_bit(bit, own, other, axis=0):
    own, other = jnp.expand_dims(own, axis), jnp.expand_dims(other, axis)
    return jnp.where(
        bit == 0,
        jnp.concatenate([own, other], axis=axis),
        jnp.concatenate([other, own], axis=axis),
    )


def crossed(value, axis_name, masks):
    count = lax.axis_size(axis_name)
    pairs = [(source, source ^ masks[source % len(masks)]) for source in range(count)]
    return moved(value, axis_name, pairs)


CORE = (1,)
FIRST = (2, 4)
SECOND = (4, 2)


def chip_masks(core):
    first = jnp.where(core == 0, 1, 2)
    return first, 3 - first


def gather_rows(shard):
    return lax.all_gather(shard, "dp", axis=0, tiled=True)


def picked(values, position, axis=0):
    return lax.dynamic_index_in_dim(values, position, axis, keepdims=False)


def plus(left, right):
    return (left.astype(WIDE) + right.astype(WIDE)).astype(LOW)


def summed(*parts):
    return sum([part.astype(WIDE) for part in parts]).astype(LOW)


class Chain:
    def __init__(self, steps):
        self.steps = steps
        self.pending = next(steps)
        self.result = None

    def step(self):
        if self.result is None:
            try:
                self.pending = self.steps.send(self.pending)
            except StopIteration as stop:
                self.result = stop.value

    def advance(self):
        if self.result is None:
            self.pending = timeline.hold(self.pending)
            self.step()


def pumped(values, *chains):
    live = [chain for chain in chains if chain.result is None]
    values, arrived = lax.optimization_barrier((values, [chain.pending for chain in live]))
    for chain, brought in zip(live, arrived):
        chain.pending = brought
        chain.step()
    return values


def finished(*chains, ahead=()):
    for chain in ahead:
        chain.advance()
    while any(chain.result is None for chain in chains):
        for chain in chains:
            chain.advance()
    return [chain.result for chain in chains]


def places_steps(sums):
    half = sums.shape[0] // 2
    even = lax.axis_index("seq") % 2 == 0
    low, high = sums[:half], sums[half:]
    brought = yield crossed(jnp.where(even, high, low), "seq", (1,))
    own = plus(jnp.where(even, low, high), brought)
    own = plus(own, (yield crossed(own, "seq", (2,))))
    other = yield crossed(own, "seq", (1,))
    return jnp.concatenate([jnp.where(even, own, other), jnp.where(even, other, own)], axis=0)


def offloaded_steps(gradient):
    share = yield lax.psum_scatter(gradient, "dp", scatter_dimension=0, tiled=True)
    if lax.axis_size("dp") != 8 or lax.axis_size("seq") != 4:
        return (yield lax.psum(share, "seq")).astype(WIDE)
    return (yield from places_steps(share)).astype(WIDE)


def slot_steps(keep, send):
    core = yield crossed(send, "dp", CORE)
    one = yield crossed(summed(keep[2:], core[2:]), "dp", FIRST)
    two = yield crossed(summed(keep[1], core[1], one[1]), "dp", SECOND)
    share = summed(keep[0], core[0], one[0], two)
    return (yield from places_steps(share)).astype(WIDE)


def slot_places():
    index = lax.axis_index("dp")
    core, chip = index % 2, index // 2

    def slots(core):
        first, second = chip_masks(core)
        away = jnp.arange(4) ^ chip
        return jnp.where(away == 0, 0, jnp.where(away == second, 1, jnp.where(away == first, 2, 3)))

    places = jnp.concatenate([core[None], slots(core), slots(1 - core)])
    return places.astype(jnp.int32)


def gather_small(values):
    if lax.axis_size("dp") != 8:
        return lax.all_gather(values, "dp", axis=0)
    index = lax.axis_index("dp")
    out = by_bit(index % 2, values, crossed(values, "dp", CORE))
    out = by_bit(index // 2 % 2, out, crossed(out, "dp", (2,)))
    out = by_bit(index // 4, out, crossed(out, "dp", (4,)))
    return out.reshape((8,) + values.shape)


def small_steps(values):
    if lax.axis_size("dp") != 8 or lax.axis_size("seq") != 4:
        return (yield lax.psum(values, ("dp", "seq")))
    for axis_name, mask in (("dp", 1), ("dp", 2), ("dp", 4), ("seq", 1), ("seq", 2)):
        values = values + (yield crossed(values, axis_name, (mask,)))
    return values


def gather_steps(values):
    if lax.axis_size("seq") != 4:
        return (yield lax.all_gather(values, "seq", axis=0))
    place = lax.axis_index("seq")
    out = by_bit(place % 2, values, (yield crossed(values, "seq", (1,))))
    out = by_bit(place // 2, out, (yield crossed(out, "seq", (2,))))
    return out.reshape((4,) + values.shape)


def chunk_steps(values):
    if lax.axis_size("seq") != 4:
        return (yield lax.psum_scatter(values, "seq", scatter_dimension=0, tiled=False)).astype(WIDE)
    place = lax.axis_index("seq")
    low_bit, high_bit = place % 2, place // 2
    values = values.reshape((2, 2) + values.shape[1:])
    going = picked(values, 1 - low_bit, 1)
    values = plus(picked(values, low_bit, 1), (yield crossed(going, "seq", (1,))))
    going = picked(values, 1 - high_bit)
    return picked(values, high_bit).astype(WIDE) + (yield crossed(going, "seq", (2,))).astype(WIDE)


def interleaved(keys_values):
    rows, columns = keys_values.shape
    view = keys_values.reshape(rows, 2, columns // (2 * PAIR), PAIR)
    return view.transpose(0, 2, 1, 3).reshape(rows, columns)


def deinterleaved(keys_values):
    rows, columns = keys_values.shape
    view = keys_values.reshape(rows, columns // (2 * PAIR), 2, PAIR)
    return view.transpose(0, 2, 1, 3).reshape(rows, columns)


def local(
    tokens,
    encoded,
    cotangent,
    attn_in,
    attn_out,
    cross_in,
    cross_out,
    ffn_in,
    ffn_out,
    gains,
    biases,
    bias_ff,
    block_ids,
    enc_lengths,
):
    groups = lax.axis_size("seq")
    shards = lax.axis_size("dp")
    place = lax.axis_index("seq")
    owner = lax.axis_index("dp")
    batch, local_len, width = tokens.shape
    enc_local = encoded.shape[1]
    rows = batch * local_len
    length = local_len * groups
    enc_length = enc_local * groups
    hidden_width = ffn_in.shape[1]
    slotted = shards == 8 and groups == 4
    places = slot_places() if slotted else jnp.zeros((9,), jnp.int32)

    attn_q, attn_kv = attn_in[:, :width], interleaved(attn_in[:, width:])
    cross_q, cross_kv = cross_in[:, :width], interleaved(cross_in[:, width:])
    early = gather_rows(
        jnp.concatenate([attn_q, attn_kv, attn_out, cross_q, cross_kv, cross_out], axis=1)
    )
    slots = gathered_back(tokens, groups)
    small = jnp.concatenate([gains, biases, bias_ff.reshape(-1, gains.shape[1])], axis=0)
    small = gather_small(small)
    small = small.astype(WIDE)
    gain_rows = gains.shape[0]
    bias_rows = biases.shape[0]
    vectors = small[:, : gain_rows + bias_rows].transpose(1, 0, 2).reshape(-1, width)
    gain_all = vectors[:gain_rows]
    bias_all = vectors[gain_rows:]
    bias_hidden = small[:, gain_rows + bias_rows :].reshape(hidden_width)
    blank = jnp.zeros((width,), WIDE)
    value_bias = interleaved(jnp.concatenate([blank, bias_all[1]])[None])
    cross_value_bias = interleaved(jnp.concatenate([blank, bias_all[4]])[None])

    chunks = block_ids.reshape(batch, groups, local_len)
    order = (place - jnp.arange(groups)) % groups
    kid = jnp.take(chunks, order, axis=1).reshape(batch, length)
    qid = kid[:, :local_len]
    enc_kid = jnp.broadcast_to(jnp.arange(enc_length, dtype=jnp.int32)[None], (batch, enc_length))
    enc_qid = jnp.broadcast_to(enc_lengths[:, None] - 1, (batch, local_len))
    ids = (kid[:, None, :], kid[:, :, None], qid[:, None, :], qid[:, :, None])
    enc_ids = (enc_kid[:, None, :], enc_kid[:, :, None], enc_qid[:, None, :], enc_qid[:, :, None])

    vectors = (gain_all, bias_all, bias_hidden, value_bias, cross_value_bias)
    early, slots, vectors, ids, enc_ids = lax.optimization_barrier(
        (early, slots, vectors, ids, enc_ids)
    )
    gain_all, bias_all, bias_hidden, value_bias, cross_value_bias = vectors
    attn_q, attn_kv = early[:, :width], early[:, width : 3 * width]
    attn_out, cross_q = early[:, 3 * width : 4 * width], early[:, 4 * width : 5 * width]
    cross_kv = early[:, 5 * width : 7 * width]
    ffn_in = gather_rows(ffn_in)
    ffn_out = gather_rows(ffn_out)
    enc_gather = Chain(gather_steps(tied(encoded, slots[-1])))

    token_each = [
        jnp.concatenate([slot[number] for slot in slots], axis=0) for number in range(batch)
    ]
    token_flat = tokens.reshape(rows, width)
    queries = (product(token_flat, attn_q) + bias_all[0]).astype(LOW)
    queries = queries.reshape(batch, local_len, width)
    keys_values = jnp.stack(
        [(product(each, attn_kv) + value_bias).astype(LOW) for each in token_each]
    )

    queries, keys_values = pumped((queries, keys_values), enc_gather)
    context, totals = attend_forward(queries, keys_values, ids)
    context = pumped(context, enc_gather)
    encoded = enc_gather.result
    enc_all = encoded.transpose(1, 0, 2, 3).reshape(batch * enc_length, width)
    enc_kv = (product(enc_all, cross_kv) + cross_value_bias).astype(LOW)
    enc_kv = enc_kv.reshape(batch, enc_length, 2 * width)
    context_flat = context.reshape(rows, width)
    first_sum = token_flat.astype(WIDE) + product(context_flat, attn_out) + bias_all[2]
    first = layer_norm(first_sum, gain_all[0], bias_all[7])
    first_low = first.astype(LOW)
    cross_queries = (product(first_low, cross_q) + bias_all[3]).astype(LOW)
    cross_queries = cross_queries.reshape(batch, local_len, width)
    cross_context, cross_totals = attend_forward(cross_queries, enc_kv, enc_ids)
    cross_flat = cross_context.reshape(rows, width)
    stage_vectors = jnp.stack(
        [bias_all[5], gain_all[1], bias_all[8], bias_all[6], gain_all[2], bias_all[9]]
    )
    final, d_second_sum, d_cross_ctx, sums, d_bias_hidden, *grads = ffn_stage(
        places,
        first,
        cross_flat,
        cotangent.reshape(rows, width),
        stage_vectors,
        bias_hidden[None],
        early,
        ffn_in,
        ffn_out,
        slotted,
    )
    if slotted:
        out_chain = Chain(slot_steps(*grads[2:]))
        in_chain = Chain(slot_steps(*grads[:2]))
    else:
        out_chain = Chain(offloaded_steps(grads[1]))
        in_chain = Chain(offloaded_steps(grads[0]))

    def gradient_chain(groups, after, extra=()):
        if slotted:
            products = slotted_products(places, groups, extra)
            products, after = lax.optimization_barrier((products, after))
            return Chain(slot_steps(*products)), after
        gradient, after = lax.optimization_barrier((plain_products(groups), after))
        return Chain(offloaded_steps(gradient)), after

    d_cross_ctx = d_cross_ctx.reshape(cross_context.shape)
    d_cross_q, d_enc = attend_backward(
        cross_queries, enc_kv, enc_ids, cross_context, d_cross_ctx, cross_totals, 0, batch
    )
    d_cross_q, d_enc = pumped((d_cross_q, d_enc), out_chain, in_chain)
    d_cross_q = d_cross_q.reshape(rows, width)
    d_enc = d_enc.reshape(-1, 2 * width)
    d_encoded = right_transposed(d_enc, cross_kv)
    d_encoded = d_encoded.reshape(batch, groups, enc_local, width).astype(LOW)
    d_encoded, d_cross_q = lax.optimization_barrier((d_encoded, d_cross_q))
    enc_chain = Chain(chunk_steps(d_encoded.transpose(1, 0, 2, 3)))
    d_first = d_second_sum + right_transposed(d_cross_q, cross_q)
    d_first_sum, d_gain_one, d_offset_one = norm_backward(first_sum, gain_all[0], d_first)
    d_attn = d_first_sum.astype(LOW)
    d_context = right_transposed(d_attn, attn_out).astype(LOW).reshape(context.shape)
    d_context = pumped(d_context, out_chain, enc_chain)
    left = (context_flat, first_low, enc_all, d_attn, d_cross_q, d_enc)
    left, d_context = lax.optimization_barrier((left, d_context))
    mid_chain, d_context = gradient_chain([[pair] for pair in zip(left[:3], left[3:])], d_context)

    def token_chain(d_kv, after):
        d_part = right_transposed(d_kv, attn_kv).astype(LOW)
        d_part, after = lax.optimization_barrier((d_part, after))
        d_part = d_part.reshape(groups, local_len, width)
        return Chain(scatter_steps(list(d_part), groups)), after

    d_query, d_key_value, token_chains = [], [], []
    for number in range(batch):
        d_q, d_kv = attend_backward(
            queries, keys_values, ids, context, d_context, totals, number, 1
        )
        pumps = (out_chain, in_chain, mid_chain, enc_chain)[: 2 if number else 4]
        d_q, d_kv, d_context = pumped((d_q[0], d_kv[0], d_context), *pumps)
        d_query.append(d_q)
        chain, (d_kv, d_context) = token_chain(d_kv, (d_kv, d_context))
        token_chains.append(chain)
        d_key_value.append(d_kv)
    part = width // shards
    hidden_rows = d_bias_hidden.reshape(shards, -1, part).transpose(1, 0, 2).reshape(-1, width)
    vectors = gain_rows + bias_rows + hidden_rows.shape[0]
    query_rows = column_total(jnp.concatenate(d_query, axis=0))[None]
    singles = [d_gain_one[None], query_rows]
    singles += [column_total(d_context.reshape(rows, width))[None], column_total(d_attn)[None]]
    singles += [column_total(d_cross_q)[None], d_offset_one[None]]
    extra = [(one, 0, at, 1) for one, at in zip(singles, (0, 3, 4, 5, 6, 10))]
    extra += [(sums, row, at, 1) for row, at in enumerate((2, 12, 9, 1, 11, 8, 7))]
    extra.append((hidden_rows, 0, gain_rows + bias_rows, hidden_rows.shape[0]))
    query_rows = jnp.concatenate(d_query, axis=0)
    query_rows, d_query, d_key_value = lax.optimization_barrier((query_rows, d_query, d_key_value))
    attn_chain, (query_rows, d_key_value) = gradient_chain(
        [
            list(zip([tokens[number] for number in range(batch)], d_query)),
            list(zip(token_each, d_key_value)),
        ],
        (query_rows, d_key_value),
        extra,
    )
    query_rows, d_key_value = pumped(
        (query_rows, d_key_value), mid_chain, out_chain, token_chains[0]
    )
    query_rows = pumped(query_rows, attn_chain, in_chain, token_chains[-1])
    d_tokens = d_first_sum + right_transposed(query_rows, attn_q)
    timeline.token = d_tokens.reshape(tokens.shape)
    early, late = token_chains[0], token_chains[-1]
    ahead = [mid_chain, attn_chain, out_chain, early, in_chain, attn_chain, mid_chain]
    ahead += [attn_chain, in_chain, mid_chain, attn_chain, late, mid_chain, attn_chain]
    chains = [attn_chain, mid_chain, in_chain, out_chain, enc_chain]
    grad_attn, middle, grad_in, grad_ffn_out, d_encoded, *d_parts = finished(
        *chains, *token_chains, ahead=ahead
    )
    d_tokens, timeline.token = timeline.token, None
    d_tokens = d_tokens + jnp.stack(d_parts)
    if slotted:
        mine = grad_attn[:, 3 * width :].T
    else:
        vector_grads = jnp.zeros((vectors, width), WIDE)
        for value, first, at, count in extra:
            vector_grads = vector_grads.at[at : at + count].set(value[first : first + count])
        (vector_grads,) = finished(Chain(small_steps(vector_grads)))
        mine = lax.dynamic_slice_in_dim(vector_grads, owner * part, part, axis=1)
    grad_cross_out = grad_in[:, hidden_width:]
    return (
        final.reshape(batch, local_len, width),
        d_tokens,
        d_encoded,
        grad_attn[:, : 3 * width],
        middle[:, :width],
        middle[:, width : 4 * width],
        grad_cross_out,
        grad_in[:, :hidden_width],
        grad_ffn_out,
        mine[:gain_rows],
        mine[gain_rows : gain_rows + bias_rows],
        mine[gain_rows + bias_rows : vectors].reshape(-1),
    )


def solution(mesh):
    split = P("dp", "seq", None)
    rows = P("dp", None)
    columns = P(None, "dp")
    vector = P("dp")
    in_specs = (split,) * 3 + (rows,) * 6 + (columns, columns, vector, rows, vector)
    out_specs = (split,) * 3 + (rows,) * 6 + (columns, columns, vector)
    return jax.shard_map(local, mesh=mesh, in_specs=in_specs, out_specs=out_specs, check_vma=False)
```

```python
import jax
import jax.numpy as jnp
from jax import lax
from jax.experimental import pallas as pl
from jax.experimental.pallas import tpu as pltpu
from jax.sharding import PartitionSpec as P

HD = 64
PAIR = 2 * HD
EPSILON = 1e-05
MASKED = -1e30
LOW = jnp.bfloat16
WIDE = jnp.float32


def product(left, right):
    return jnp.dot(left, right, preferred_element_type=WIDE)


def left_transposed(left, right):
    return lax.dot_general(left, right, (((0,), (0,)), ((), ())), preferred_element_type=WIDE)


def right_transposed(left, right):
    return lax.dot_general(left, right, (((1,), (1,)), ((), ())), preferred_element_type=WIDE)


def column_total(values):
    return jnp.sum(values.astype(WIDE), axis=0)


def layer_norm(summed, gain, offset):
    centre = summed - jnp.mean(summed, axis=-1, keepdims=True)
    spread = jnp.mean(centre * centre, axis=-1, keepdims=True)
    return centre * lax.rsqrt(spread + EPSILON) * gain + offset


def norm_backward(summed, gain, upstream):
    centre = summed - jnp.mean(summed, axis=-1, keepdims=True)
    spread = jnp.mean(centre * centre, axis=-1, keepdims=True)
    inverse = lax.rsqrt(spread + EPSILON)
    unit = centre * inverse
    scaled = upstream * gain
    mean_scaled = jnp.mean(scaled, axis=-1, keepdims=True)
    mean_both = jnp.mean(scaled * unit, axis=-1, keepdims=True)
    d_summed = (scaled - mean_scaled - unit * mean_both) * inverse
    return d_summed, jnp.sum(upstream * unit, axis=0), jnp.sum(upstream, axis=0)


def stacked_heads(values):
    lane = lax.broadcasted_iota(jnp.int32, values.shape, 1)
    none = jnp.zeros_like(values)
    return jnp.concatenate(
        [jnp.where(lane < HD, values, none), jnp.where(lane >= HD, values, none)], axis=0
    )


def merged_heads(stacked):
    half = stacked.shape[0] // 2
    lane = lax.broadcasted_iota(jnp.int32, (half, PAIR), 1)
    return jnp.where(lane < HD, stacked[:half], stacked[half:])


def forward_kernel(q_ref, kv_ref, qid_ref, kid_ref, o_ref, total_ref):
    queries = stacked_heads(q_ref[0]) * jnp.asarray(HD**-0.5, LOW)
    scores = right_transposed(queries, kv_ref[0, :, :PAIR])
    qid = qid_ref[0]
    allowed = kid_ref[0] <= jnp.concatenate([qid, qid], axis=0)
    scores = jnp.where(allowed, scores, MASKED)
    highest = jnp.max(scores, axis=-1, keepdims=True)
    exponent = jnp.exp(scores - highest)
    denominator = jnp.sum(exponent, axis=-1, keepdims=True)
    context = product(exponent.astype(LOW), kv_ref[0, :, PAIR:]) / denominator
    o_ref[0] = merged_heads(context).astype(LOW)
    totals = highest + jnp.log(denominator)
    total_ref[0, 0] = jnp.transpose(jnp.broadcast_to(totals, (totals.shape[0], 128)))[:8]


def backward_kernel(q_ref, kv_ref, qid_ref, kid_ref, o_ref, do_ref, total_ref, dq_ref, dkv_ref):
    queries = stacked_heads(q_ref[0]) * jnp.asarray(HD**-0.5, LOW)
    upstream = stacked_heads(do_ref[0])
    both = do_ref[0].astype(WIDE) * o_ref[0].astype(WIDE)
    row = lax.broadcasted_iota(jnp.int32, (8, PAIR), 0)
    lane = lax.broadcasted_iota(jnp.int32, (8, PAIR), 1)
    pick = jnp.where(lane // HD == row, 1.0, 0.0).astype(WIDE)
    inner = lax.dot_general(
        pick,
        both,
        (((1,), (1,)), ((), ())),
        precision=lax.Precision.HIGHEST,
        preferred_element_type=WIDE,
    )
    inner = jnp.concatenate([inner[0:1], inner[1:2]], axis=1)
    keys = kv_ref[0, :, :PAIR]
    qid = qid_ref[0]
    allowed = kid_ref[0] <= jnp.concatenate([qid, qid], axis=1)
    scores = jnp.where(allowed, right_transposed(keys, queries), MASKED)
    weights = jnp.exp(scores - total_ref[0, 0, 0:1])
    dkv_ref[0, :, PAIR:] = product(weights.astype(LOW), upstream).astype(LOW)
    weight_grads = right_transposed(kv_ref[0, :, PAIR:], upstream)
    score_grads = (weights * (weight_grads - inner)).astype(LOW)
    dkv_ref[0, :, :PAIR] = product(score_grads, queries).astype(LOW)
    dq = left_transposed(score_grads, keys) * (HD**-0.5)
    dq_ref[0] = merged_heads(dq).astype(LOW)


def attend_forward(queries, keys_values, ids):
    batch, rows, width = queries.shape
    keys = keys_values.shape[1]
    pairs = width // PAIR
    one = pl.BlockSpec((1, rows, PAIR), lambda b, p: (b, 0, p))
    work = batch * pairs * rows * keys
    return pl.pallas_call(
        forward_kernel,
        grid=(batch, pairs),
        in_specs=[
            one,
            pl.BlockSpec((1, keys, 2 * PAIR), lambda b, p: (b, 0, p)),
            pl.BlockSpec((1, rows, 1), lambda b, p: (b, 0, 0)),
            pl.BlockSpec((1, 1, keys), lambda b, p: (b, 0, 0)),
        ],
        out_specs=[one, pl.BlockSpec((1, 1, 8, 2 * rows), lambda b, p: (b, p, 0, 0))],
        out_shape=[
            jax.ShapeDtypeStruct((batch, rows, width), LOW),
            jax.ShapeDtypeStruct((batch, pairs, 8, 2 * rows), WIDE),
        ],
        cost_estimate=pl.CostEstimate(
            flops=4000 * work, transcendentals=2 * work, bytes_accessed=8 * batch * keys * width
        ),
        name="attend_forward",
    )(queries, keys_values, ids[3], ids[0])


def attend_backward(queries, keys_values, ids, context, upstream, totals, start, count):
    _, rows, width = queries.shape
    keys = keys_values.shape[1]
    pairs = width // PAIR
    one = pl.BlockSpec((1, rows, PAIR), lambda b, p: (start + b, 0, p))
    work = count * pairs * rows * keys
    return pl.pallas_call(
        backward_kernel,
        grid=(count, pairs),
        in_specs=[
            one,
            pl.BlockSpec((1, keys, 2 * PAIR), lambda b, p: (start + b, 0, p)),
            pl.BlockSpec((1, 1, rows), lambda b, p: (start + b, 0, 0)),
            pl.BlockSpec((1, keys, 1), lambda b, p: (start + b, 0, 0)),
            one,
            one,
            pl.BlockSpec((1, 1, 8, 2 * rows), lambda b, p: (start + b, p, 0, 0)),
        ],
        out_specs=[
            pl.BlockSpec((1, rows, PAIR), lambda b, p: (b, 0, p)),
            pl.BlockSpec((1, keys, 2 * PAIR), lambda b, p: (b, 0, p)),
        ],
        out_shape=[
            jax.ShapeDtypeStruct((count, rows, width), LOW),
            jax.ShapeDtypeStruct((count, keys, 2 * width), LOW),
        ],
        cost_estimate=pl.CostEstimate(
            flops=4000 * work, transcendentals=2 * work, bytes_accessed=8 * count * keys * width
        ),
        name="attend_backward",
    )(queries, keys_values, ids[2], ids[1], context, upstream, totals)


CHUNK = 768


def normalised(summed):
    centre = summed - jnp.mean(summed, axis=-1, keepdims=True)
    inverse = lax.rsqrt(jnp.mean(centre * centre, axis=-1, keepdims=True) + EPSILON)
    return centre * inverse, inverse


def normalised_backward(unit, inverse, scaled):
    mean_scaled = jnp.mean(scaled, axis=-1, keepdims=True)
    mean_both = jnp.mean(scaled * unit, axis=-1, keepdims=True)
    return (scaled - mean_scaled - unit * mean_both) * inverse


def gelu_pair(values):
    size = jnp.abs(values) * (0.5**0.5)
    bell = jnp.exp(-0.5 * values * values)
    t = 1.0 / (1.0 + 0.3275911 * size)
    series = t * (
        0.127414796
        + t * (-0.142248368 + t * (0.7107068705 + t * (-0.7265760135 + t * 0.5307027145)))
    )
    tail = series * bell
    below = jnp.where(values >= 0, 1.0 - tail, tail)
    return values * below, below + values * bell * 0.3989422804014327


def total_row(values):
    return jnp.sum(values, axis=0, keepdims=True)


def slot_copies(source, keep_ref, send_ref, place_ref, semaphores, columns=None, chips=None):
    rows = keep_ref.shape[1]
    core = place_ref[0]
    found = []
    for chip in range(4) if chips is None else chips:
        for number, (slots_ref, owner) in enumerate(((keep_ref, core), (send_ref, 1 - core))):
            at = pl.ds(pl.multiple_of((2 * chip + owner) * rows, 16), rows)
            slot = place_ref[1 + 4 * number + chip]
            taken, given = source.at[at], slots_ref.at[slot]
            if columns is not None:
                taken, given = source.at[at, columns], slots_ref.at[slot, :, columns]
            found.append(pltpu.make_async_copy(taken, given, semaphores.at[2 * chip + number]))
    return found


def ffn_kernel(
    place_ref,
    first_ref,
    cross_ref,
    cot_ref,
    vector_ref,
    hidden_bias_ref,
    early_ref,
    in_ref,
    out_ref,
    final_ref,
    d_sum_ref,
    d_ctx_ref,
    sums_ref,
    hidden_sums_ref,
    *others,
):
    grad_refs, scratch = others[:-14], others[-14:]
    w_cross, w_in, w_out, hidden, slope, total, low, d_low, g_in, g_out = scratch[:10]
    load_sem, out_sem, in_sem, cross_sem = scratch[10:14]
    rows, width = first_ref.shape
    hidden_width = w_in.shape[1]
    count = hidden_width // CHUNK
    slotted = len(grad_refs) == 4
    cross_at = early_ref.shape[1] - width
    loads = [
        pltpu.make_async_copy(early_ref.at[:, cross_at:], w_cross, load_sem.at[0]),
        pltpu.make_async_copy(in_ref, w_in, load_sem.at[1]),
        pltpu.make_async_copy(out_ref, w_out, load_sem.at[2]),
    ]
    for load in loads:
        load.start()
    loads[0].wait()
    second_sum = first_ref[...] + product(cross_ref[...], w_cross[...]) + vector_ref[0:1]
    unit, inverse = normalised(second_sum)
    second = unit * vector_ref[1:2] + vector_ref[2:3]
    low[...] = second.astype(LOW)
    total[...] = second + vector_ref[3:4]
    d_sum_ref[...] = unit
    loads[1].wait()
    loads[2].wait()

    def forward(step, carry):
        at = pl.ds(pl.multiple_of(step * CHUNK, CHUNK), CHUNK)
        activation = product(low[...], w_in[:, at]) + hidden_bias_ref[:, at]
        value, slope_value = gelu_pair(activation)
        value = value.astype(LOW)
        hidden[:, at] = value
        slope[:, at] = slope_value
        total[...] += product(value, w_out[at, :])
        return carry

    lax.fori_loop(0, count, forward, 0)
    third, third_inverse = normalised(total[...])
    final_ref[...] = (third * vector_ref[4:5] + vector_ref[5:6]).astype(LOW)
    upstream = cot_ref[...].astype(WIDE)
    sums_ref[0:1] = total_row(upstream * third)
    sums_ref[1:2] = total_row(upstream)
    d_third = normalised_backward(third, third_inverse, upstream * vector_ref[4:5])
    d_low[...] = d_third.astype(LOW)
    sums_ref[2:3] = total_row(d_low[...].astype(WIDE))
    total[...] = d_third

    def backward(step, carry):
        at = pl.ds(pl.multiple_of(step * CHUNK, CHUNK), CHUNK)
        g_out[at, :] = left_transposed(hidden[:, at], d_low[...]).astype(LOW)
        d_hidden = right_transposed(d_low[...], w_out[at, :])
        d_activation = (d_hidden * slope[:, at]).astype(LOW)
        hidden_sums_ref[:, at] = total_row(d_activation.astype(WIDE))
        g_in[:, at] = left_transposed(low[...], d_activation).astype(LOW)
        total[...] += right_transposed(d_activation, w_in[:, at])
        if slotted:
            for copy in slot_copies(g_out, *grad_refs[2:], place_ref, out_sem, None, [step]):
                copy.start()
        return carry

    lax.fori_loop(0, count, backward, 0)
    if slotted:
        copies = [
            slot_copies(g_out, *grad_refs[2:], place_ref, out_sem),
            slot_copies(
                g_in, *grad_refs[:2], place_ref, in_sem, pl.ds(0, hidden_width)
            ),
            slot_copies(
                g_in, *grad_refs[:2], place_ref, cross_sem, pl.ds(hidden_width, width)
            ),
        ]
    else:
        copies = [
            [pltpu.make_async_copy(g_out, grad_refs[1], out_sem.at[0])],
            [pltpu.make_async_copy(g_in, grad_refs[0], in_sem.at[0])],
        ]
        copies[0][0].start()
    if slotted:
        for copy in copies[1]:
            copy.start()
    d_second = total[...]
    unit = d_sum_ref[...]
    sums_ref[3:4] = total_row(d_second * unit)
    sums_ref[4:5] = total_row(d_second)
    d_second_sum = normalised_backward(unit, inverse, d_second * vector_ref[1:2])
    d_sum_ref[...] = d_second_sum
    d_cross = d_second_sum.astype(LOW)
    sums_ref[5:6] = total_row(d_cross.astype(WIDE))
    g_in[:, hidden_width:] = left_transposed(cross_ref[...], d_cross).astype(LOW)
    for copy in copies[-1]:
        copy.start()
    d_ctx = right_transposed(d_cross, w_cross[...]).astype(LOW)
    d_ctx_ref[...] = d_ctx
    sums_ref[6:7] = total_row(d_ctx.astype(WIDE))
    sums_ref[7:8] = jnp.zeros_like(sums_ref[7:8])
    for group in copies:
        for copy in group:
            copy.wait()


def ffn_stage(
    places, first, cross, cotangent, vectors, hidden_bias, early, ffn_in, ffn_out, slotted
):
    rows, width = first.shape
    hidden_width = ffn_in.shape[1]
    count = hidden_width // CHUNK
    inside = pl.BlockSpec(memory_space=pltpu.VMEM)
    outside = pl.BlockSpec(memory_space=pl.ANY)
    grads = [(width, hidden_width + width), (hidden_width, width)]
    if slotted:
        grads = [(4, shape[0] // 8, shape[1]) for shape in grads for _ in range(2)]
    return pl.pallas_call(
        ffn_kernel,
        in_specs=[pl.BlockSpec(memory_space=pltpu.SMEM)] + [inside] * 5 + [outside] * 3,
        out_specs=[inside] * 5 + [outside] * len(grads),
        out_shape=[
            jax.ShapeDtypeStruct((rows, width), LOW),
            jax.ShapeDtypeStruct((rows, width), WIDE),
            jax.ShapeDtypeStruct((rows, width), LOW),
            jax.ShapeDtypeStruct((8, width), WIDE),
            jax.ShapeDtypeStruct((1, hidden_width), WIDE),
        ]
        + [jax.ShapeDtypeStruct(shape, LOW) for shape in grads],
        scratch_shapes=[
            pltpu.VMEM((width, width), LOW),
            pltpu.VMEM((width, hidden_width), LOW),
            pltpu.VMEM((hidden_width, width), LOW),
            pltpu.VMEM((rows, hidden_width), LOW),
            pltpu.VMEM((rows, hidden_width), WIDE),
            pltpu.VMEM((rows, width), WIDE),
            pltpu.VMEM((rows, width), LOW),
            pltpu.VMEM((rows, width), LOW),
            pltpu.VMEM((width, hidden_width + width), LOW),
            pltpu.VMEM((hidden_width, width), LOW),
            pltpu.SemaphoreType.DMA((3,)),
            pltpu.SemaphoreType.DMA((8,)),
            pltpu.SemaphoreType.DMA((8,)),
            pltpu.SemaphoreType.DMA((8,)),
        ],
        compiler_params=pltpu.CompilerParams(vmem_limit_bytes=58 << 20),
        cost_estimate=pl.CostEstimate(
            flops=16 * rows * width * hidden_width,
            transcendentals=rows * hidden_width,
            bytes_accessed=12 * width * hidden_width,
        ),
        name="ffn_stage",
    )(places, first, cross, cotangent, vectors, hidden_bias, early, ffn_in, ffn_out)


def apart(start, width):
    pair, half = divmod(start // PAIR, 2)
    return half * width + pair * PAIR


def slotted_products(places, groups, extra=()):
    arrays = [value for group in groups for pair in group for value in pair]
    width = arrays[0].shape[1]
    widths = [group[0][1].shape[1] for group in groups]
    columns = sum(widths) + (128 if extra else 0)
    extras = [part[0] for part in extra]

    def kernel(place_ref, *refs):
        inputs, refs = refs[: len(arrays)], refs[len(arrays) :]
        extra_refs, refs = refs[: len(extras)], refs[len(extras) :]
        keep_ref, send_ref = refs[:2]
        buffers, (rows_ref, total, load_sem, store_sem) = refs[2:-4], refs[-4:]
        loads = [
            pltpu.make_async_copy(inputs[number], buffers[number], load_sem.at[number])
            for number in range(len(arrays))
        ]
        for load in loads:
            load.start()
        copies = []

        def leave(number, at, size):
            group = slot_copies(
                total, keep_ref, send_ref, place_ref, store_sem.at[number], pl.ds(at, size)
            )
            for copy in group:
                copy.start()
            copies.extend(group)

        at = number = 0
        for index, group in enumerate(groups):
            value = None
            for _ in group:
                loads[number].wait()
                loads[number + 1].wait()
                term = left_transposed(buffers[number][...], buffers[number + 1][...])
                value = term if value is None else value + term
                number += 2
            value = value.astype(LOW)
            for start in range(0, widths[index], PAIR):
                given = at + (start if widths[index] == width else apart(start, width))
                total[:, given : given + PAIR] = value[:, start : start + PAIR]
            leave(index, at, widths[index])
            at += widths[index]
        if extras:
            rows_ref[...] = jnp.zeros_like(rows_ref)
            for extra_ref, (_, first, given, count) in zip(extra_refs, extra):
                rows_ref[given : given + count] = extra_ref[first : first + count]
            total[:, at:] = jnp.transpose(rows_ref[...]).astype(LOW)
            leave(len(groups), at, columns - at)
        for copy in copies:
            copy.wait()

    outside = pl.BlockSpec(memory_space=pl.ANY)
    shape = jax.ShapeDtypeStruct((4, width // 8, columns), LOW)
    return pl.pallas_call(
        kernel,
        in_specs=[pl.BlockSpec(memory_space=pltpu.SMEM)]
        + [outside] * len(arrays)
        + [pl.BlockSpec(memory_space=pltpu.VMEM)] * len(extras),
        out_specs=[outside] * 2,
        out_shape=[shape] * 2,
        scratch_shapes=[pltpu.VMEM(value.shape, LOW) for value in arrays]
        + [
            pltpu.VMEM((128, width), WIDE),
            pltpu.VMEM((width, columns), LOW),
            pltpu.SemaphoreType.DMA((len(arrays),)),
            pltpu.SemaphoreType.DMA((len(groups) + 1, 8)),
        ],
        compiler_params=pltpu.CompilerParams(vmem_limit_bytes=58 << 20),
        cost_estimate=pl.CostEstimate(
            flops=2 * width * sum(left.size // width * right.shape[1]
                                  for group in groups for left, right in group),
            transcendentals=0,
            bytes_accessed=sum(2 * value.size for value in arrays) + 2 * width * columns,
        ),
        name="slotted_products",
    )(places, *arrays, *extras)


def plain_products(groups):
    found = [sum([left_transposed(*pair) for pair in group]) for group in groups]
    width = found[0].shape[1]
    found = [part if part.shape[1] == width else deinterleaved(part) for part in found]
    return jnp.concatenate([part.astype(LOW) for part in found], axis=1)


def gathered_back(own, groups):
    slots = [own]
    around = lax.ppermute(own, "seq", [(source, (source - 1) % groups) for source in range(groups)])
    for step in range(1, groups - 1):
        pairs = [(source, source + 1) for source in range(step - 1, groups - 1)]
        slots.append(lax.ppermute(slots[-1], "seq", pairs))
    return slots + [around]


def scatter_steps(slots, groups):
    ring = [(source, (source + 1) % groups) for source in range(groups)]
    if groups == 4:
        parts = [moved(slots[2], "seq", [(3, 2), (2, 1)]), moved(slots[3], "seq", ring)]
        ahead, around = yield parts
        back = [(source, source - 1) for source in range(1, groups)]
        last, around = yield [moved(plus(slots[1], ahead), "seq", back), around]
        parts = [around, last]
    else:
        parts = [moved(slots[groups - 1], "seq", ring)]
        for step in range(groups - 2, 0, -1):
            pairs = [(source, source - step) for source in range(step, groups)]
            parts.append(moved(slots[step], "seq", pairs))
        parts = yield parts
    return sum([part.astype(WIDE) for part in parts], slots[0].astype(WIDE))


def pair_steps(slots, groups):
    ring = [(source, (source + 1) % groups) for source in range(groups)]
    back = [(source, source - 1) for source in range(1, groups)]
    first = slots[0]
    ahead, around = yield [
        moved(first[2], "seq", [(3, 2), (2, 1)]),
        moved(first[groups - 1], "seq", ring),
    ]
    second = slots[1]
    going = jnp.concatenate([plus(first[1], ahead), second[2]], axis=0)
    brought, last = yield [moved(going, "seq", back), moved(second[groups - 1], "seq", ring)]
    ahead = brought[first[1].shape[0] :]
    ended = yield moved(plus(second[1], ahead), "seq", back)
    brought = brought[: first[1].shape[0]]
    return jnp.stack(
        [
            first[0].astype(WIDE) + around.astype(WIDE) + brought.astype(WIDE),
            second[0].astype(WIDE) + last.astype(WIDE) + ended.astype(WIDE),
        ]
    )


class Order:
    token = None

    def hold(self, value):
        if self.token is not None:
            self.token, value = lax.optimization_barrier((self.token, value))
        return value


timeline = Order()


def moved(value, axis_name, pairs):
    return lax.ppermute(timeline.hold(value), axis_name, pairs)


def tied(value, *others):
    return lax.optimization_barrier((value,) + others)[0]


def by_bit(bit, own, other, axis=0):
    own, other = jnp.expand_dims(own, axis), jnp.expand_dims(other, axis)
    return jnp.where(
        bit == 0,
        jnp.concatenate([own, other], axis=axis),
        jnp.concatenate([other, own], axis=axis),
    )


def crossed(value, axis_name, masks):
    count = lax.axis_size(axis_name)
    pairs = [(source, source ^ masks[source % len(masks)]) for source in range(count)]
    return moved(value, axis_name, pairs)


CORE = (1,)
FIRST = (2, 4)
SECOND = (4, 2)


def chip_masks(core):
    first = jnp.where(core == 0, 1, 2)
    return first, 3 - first


def gather_rows(shard):
    return lax.all_gather(shard, "dp", axis=0, tiled=True)


def picked(values, position, axis=0):
    return lax.dynamic_index_in_dim(values, position, axis, keepdims=False)


def plus(left, right):
    return (left.astype(WIDE) + right.astype(WIDE)).astype(LOW)


def summed(*parts):
    return sum([part.astype(WIDE) for part in parts]).astype(LOW)


class Chain:
    def __init__(self, steps):
        self.steps = steps
        self.pending = next(steps)
        self.result = None

    def step(self):
        if self.result is None:
            try:
                self.pending = self.steps.send(self.pending)
            except StopIteration as stop:
                self.result = stop.value

    def advance(self):
        if self.result is None:
            self.pending = timeline.hold(self.pending)
            self.step()


def pumped(values, *chains):
    live = [chain for chain in chains if chain.result is None]
    values, arrived = lax.optimization_barrier((values, [chain.pending for chain in live]))
    for chain, brought in zip(live, arrived):
        chain.pending = brought
        chain.step()
    return values


def finished(*chains, ahead=()):
    for chain in ahead:
        chain.advance()
    while any(chain.result is None for chain in chains):
        for chain in chains:
            chain.advance()
    return [chain.result for chain in chains]


def places_steps(sums):
    half = sums.shape[0] // 2
    even = lax.axis_index("seq") % 2 == 0
    low, high = sums[:half], sums[half:]
    brought = yield crossed(jnp.where(even, high, low), "seq", (1,))
    own = plus(jnp.where(even, low, high), brought)
    own = plus(own, (yield crossed(own, "seq", (2,))))
    other = yield crossed(own, "seq", (1,))
    return jnp.concatenate([jnp.where(even, own, other), jnp.where(even, other, own)], axis=0)


def offloaded_steps(gradient):
    share = yield lax.psum_scatter(gradient, "dp", scatter_dimension=0, tiled=True)
    if lax.axis_size("dp") != 8 or lax.axis_size("seq") != 4:
        return (yield lax.psum(share, "seq")).astype(WIDE)
    return (yield from places_steps(share)).astype(WIDE)


def slot_steps(keep, send):
    core = yield crossed(send, "dp", CORE)
    one = yield crossed(summed(keep[2:], core[2:]), "dp", FIRST)
    two = yield crossed(summed(keep[1], core[1], one[1]), "dp", SECOND)
    share = summed(keep[0], core[0], one[0], two)
    return (yield from places_steps(share)).astype(WIDE)


def slot_places():
    index = lax.axis_index("dp")
    core, chip = index % 2, index // 2

    def slots(core):
        first, second = chip_masks(core)
        away = jnp.arange(4) ^ chip
        return jnp.where(away == 0, 0, jnp.where(away == second, 1, jnp.where(away == first, 2, 3)))

    places = jnp.concatenate([core[None], slots(core), slots(1 - core)])
    return places.astype(jnp.int32)


def gather_small(values):
    if lax.axis_size("dp") != 8:
        return lax.all_gather(values, "dp", axis=0)
    index = lax.axis_index("dp")
    out = by_bit(index % 2, values, crossed(values, "dp", CORE))
    out = by_bit(index // 2 % 2, out, crossed(out, "dp", (2,)))
    out = by_bit(index // 4, out, crossed(out, "dp", (4,)))
    return out.reshape((8,) + values.shape)


def small_steps(values):
    if lax.axis_size("dp") != 8 or lax.axis_size("seq") != 4:
        return (yield lax.psum(values, ("dp", "seq")))
    for axis_name, mask in (("dp", 1), ("dp", 2), ("dp", 4), ("seq", 1), ("seq", 2)):
        values = values + (yield crossed(values, axis_name, (mask,)))
    return values


def gather_steps(values):
    if lax.axis_size("seq") != 4:
        return (yield lax.all_gather(values, "seq", axis=0))
    place = lax.axis_index("seq")
    out = by_bit(place % 2, values, (yield crossed(values, "seq", (1,))))
    out = by_bit(place // 2, out, (yield crossed(out, "seq", (2,))))
    return out.reshape((4,) + values.shape)


def chunk_steps(values):
    if lax.axis_size("seq") != 4:
        return (yield lax.psum_scatter(values, "seq", scatter_dimension=0, tiled=False)).astype(WIDE)
    place = lax.axis_index("seq")
    low_bit, high_bit = place % 2, place // 2
    values = values.reshape((2, 2) + values.shape[1:])
    going = picked(values, 1 - low_bit, 1)
    values = plus(picked(values, low_bit, 1), (yield crossed(going, "seq", (1,))))
    going = picked(values, 1 - high_bit)
    return picked(values, high_bit).astype(WIDE) + (yield crossed(going, "seq", (2,))).astype(WIDE)


def interleaved(keys_values):
    rows, columns = keys_values.shape
    view = keys_values.reshape(rows, 2, columns // (2 * PAIR), PAIR)
    return view.transpose(0, 2, 1, 3).reshape(rows, columns)


def deinterleaved(keys_values):
    rows, columns = keys_values.shape
    view = keys_values.reshape(rows, columns // (2 * PAIR), 2, PAIR)
    return view.transpose(0, 2, 1, 3).reshape(rows, columns)


def local(
    tokens,
    encoded,
    cotangent,
    attn_in,
    attn_out,
    cross_in,
    cross_out,
    ffn_in,
    ffn_out,
    gains,
    biases,
    bias_ff,
    block_ids,
    enc_lengths,
):
    groups = lax.axis_size("seq")
    shards = lax.axis_size("dp")
    place = lax.axis_index("seq")
    owner = lax.axis_index("dp")
    batch, local_len, width = tokens.shape
    enc_local = encoded.shape[1]
    rows = batch * local_len
    length = local_len * groups
    enc_length = enc_local * groups
    hidden_width = ffn_in.shape[1]
    slotted = shards == 8 and groups == 4
    places = slot_places() if slotted else jnp.zeros((9,), jnp.int32)

    attn_q, attn_kv = attn_in[:, :width], interleaved(attn_in[:, width:])
    cross_q, cross_kv = cross_in[:, :width], interleaved(cross_in[:, width:])
    early = gather_rows(
        jnp.concatenate([attn_q, attn_kv, attn_out, cross_q, cross_kv, cross_out], axis=1)
    )
    slots = gathered_back(tokens, groups)
    small = jnp.concatenate([gains, biases, bias_ff.reshape(-1, gains.shape[1])], axis=0)
    small = gather_small(small)
    small = small.astype(WIDE)
    gain_rows = gains.shape[0]
    bias_rows = biases.shape[0]
    vectors = small[:, : gain_rows + bias_rows].transpose(1, 0, 2).reshape(-1, width)
    gain_all = vectors[:gain_rows]
    bias_all = vectors[gain_rows:]
    bias_hidden = small[:, gain_rows + bias_rows :].reshape(hidden_width)
    blank = jnp.zeros((width,), WIDE)
    value_bias = interleaved(jnp.concatenate([blank, bias_all[1]])[None])
    cross_value_bias = interleaved(jnp.concatenate([blank, bias_all[4]])[None])

    chunks = block_ids.reshape(batch, groups, local_len)
    order = (place - jnp.arange(groups)) % groups
    kid = jnp.take(chunks, order, axis=1).reshape(batch, length)
    qid = kid[:, :local_len]
    enc_kid = jnp.broadcast_to(jnp.arange(enc_length, dtype=jnp.int32)[None], (batch, enc_length))
    enc_qid = jnp.broadcast_to(enc_lengths[:, None] - 1, (batch, local_len))
    ids = (kid[:, None, :], kid[:, :, None], qid[:, None, :], qid[:, :, None])
    enc_ids = (enc_kid[:, None, :], enc_kid[:, :, None], enc_qid[:, None, :], enc_qid[:, :, None])

    vectors = (gain_all, bias_all, bias_hidden, value_bias, cross_value_bias)
    early, slots, vectors, ids, enc_ids = lax.optimization_barrier(
        (early, slots, vectors, ids, enc_ids)
    )
    gain_all, bias_all, bias_hidden, value_bias, cross_value_bias = vectors
    attn_q, attn_kv = early[:, :width], early[:, width : 3 * width]
    attn_out, cross_q = early[:, 3 * width : 4 * width], early[:, 4 * width : 5 * width]
    cross_kv = early[:, 5 * width : 7 * width]
    ffn_in = gather_rows(ffn_in)
    ffn_out = gather_rows(ffn_out)
    enc_gather = Chain(gather_steps(tied(encoded, slots[-1])))

    token_each = [
        jnp.concatenate([slot[number] for slot in slots], axis=0) for number in range(batch)
    ]
    token_flat = tokens.reshape(rows, width)
    queries = (product(token_flat, attn_q) + bias_all[0]).astype(LOW)
    queries = queries.reshape(batch, local_len, width)
    keys_values = jnp.stack(
        [(product(each, attn_kv) + value_bias).astype(LOW) for each in token_each]
    )

    queries, keys_values = pumped((queries, keys_values), enc_gather)
    context, totals = attend_forward(queries, keys_values, ids)
    context = pumped(context, enc_gather)
    encoded = enc_gather.result
    enc_all = encoded.transpose(1, 0, 2, 3).reshape(batch * enc_length, width)
    enc_kv = (product(enc_all, cross_kv) + cross_value_bias).astype(LOW)
    enc_kv = enc_kv.reshape(batch, enc_length, 2 * width)
    context_flat = context.reshape(rows, width)
    first_sum = token_flat.astype(WIDE) + product(context_flat, attn_out) + bias_all[2]
    first = layer_norm(first_sum, gain_all[0], bias_all[7])
    first_low = first.astype(LOW)
    cross_queries = (product(first_low, cross_q) + bias_all[3]).astype(LOW)
    cross_queries = cross_queries.reshape(batch, local_len, width)
    cross_context, cross_totals = attend_forward(cross_queries, enc_kv, enc_ids)
    cross_flat = cross_context.reshape(rows, width)
    stage_vectors = jnp.stack(
        [bias_all[5], gain_all[1], bias_all[8], bias_all[6], gain_all[2], bias_all[9]]
    )
    final, d_second_sum, d_cross_ctx, sums, d_bias_hidden, *grads = ffn_stage(
        places,
        first,
        cross_flat,
        cotangent.reshape(rows, width),
        stage_vectors,
        bias_hidden[None],
        early,
        ffn_in,
        ffn_out,
        slotted,
    )
    if slotted:
        out_chain = Chain(slot_steps(*grads[2:]))
        in_chain = Chain(slot_steps(*grads[:2]))
    else:
        out_chain = Chain(offloaded_steps(grads[1]))
        in_chain = Chain(offloaded_steps(grads[0]))

    def gradient_chain(groups, after, extra=()):
        if slotted:
            products = slotted_products(places, groups, extra)
            products, after = lax.optimization_barrier((products, after))
            return Chain(slot_steps(*products)), after
        gradient, after = lax.optimization_barrier((plain_products(groups), after))
        return Chain(offloaded_steps(gradient)), after

    d_cross_ctx = d_cross_ctx.reshape(cross_context.shape)
    d_cross_q, d_enc = attend_backward(
        cross_queries, enc_kv, enc_ids, cross_context, d_cross_ctx, cross_totals, 0, batch
    )
    d_cross_q, d_enc = pumped((d_cross_q, d_enc), out_chain, in_chain)
    d_cross_q = d_cross_q.reshape(rows, width)
    d_enc = d_enc.reshape(-1, 2 * width)
    d_encoded = right_transposed(d_enc, cross_kv)
    d_encoded = d_encoded.reshape(batch, groups, enc_local, width).astype(LOW)
    d_encoded, d_cross_q = lax.optimization_barrier((d_encoded, d_cross_q))
    enc_chain = Chain(chunk_steps(d_encoded.transpose(1, 0, 2, 3)))
    d_first = d_second_sum + right_transposed(d_cross_q, cross_q)
    d_first_sum, d_gain_one, d_offset_one = norm_backward(first_sum, gain_all[0], d_first)
    d_attn = d_first_sum.astype(LOW)
    d_context = right_transposed(d_attn, attn_out).astype(LOW).reshape(context.shape)
    d_context = pumped(d_context, out_chain, enc_chain)
    left = (context_flat, first_low, enc_all, d_attn, d_cross_q, d_enc)
    left, d_context = lax.optimization_barrier((left, d_context))
    mid_chain, d_context = gradient_chain([[pair] for pair in zip(left[:3], left[3:])], d_context)

    def token_chain(d_kv, after):
        d_part = right_transposed(d_kv, attn_kv).astype(LOW)
        d_part, after = lax.optimization_barrier((d_part, after))
        token_slots.append(list(d_part.reshape(groups, local_len, width)))
        if not paired:
            return Chain(scatter_steps(token_slots[-1], groups)), after
        return Chain(pair_steps(token_slots, groups)) if len(token_slots) == 1 else None, after

    paired = groups == 4 and batch == 2
    d_query, d_key_value, token_chains, token_slots = [], [], [], []
    for number in range(batch):
        d_q, d_kv = attend_backward(
            queries, keys_values, ids, context, d_context, totals, number, 1
        )
        pumps = (out_chain, in_chain, mid_chain, enc_chain)[: 2 if number else 4]
        d_q, d_kv, d_context = pumped((d_q[0], d_kv[0], d_context), *pumps)
        d_query.append(d_q)
        chain, (d_kv, d_context) = token_chain(d_kv, (d_kv, d_context))
        if chain is not None:
            token_chains.append(chain)
        d_key_value.append(d_kv)
    part = width // shards
    hidden_rows = d_bias_hidden.reshape(shards, -1, part).transpose(1, 0, 2).reshape(-1, width)
    vectors = gain_rows + bias_rows + hidden_rows.shape[0]
    query_rows = column_total(jnp.concatenate(d_query, axis=0))[None]
    singles = [d_gain_one[None], query_rows]
    singles += [column_total(d_context.reshape(rows, width))[None], column_total(d_attn)[None]]
    singles += [column_total(d_cross_q)[None], d_offset_one[None]]
    extra = [(one, 0, at, 1) for one, at in zip(singles, (0, 3, 4, 5, 6, 10))]
    extra += [(sums, row, at, 1) for row, at in enumerate((2, 12, 9, 1, 11, 8, 7))]
    extra.append((hidden_rows, 0, gain_rows + bias_rows, hidden_rows.shape[0]))
    query_rows = jnp.concatenate(d_query, axis=0)
    query_rows, d_query, d_key_value = lax.optimization_barrier((query_rows, d_query, d_key_value))
    attn_chain, (query_rows, d_key_value) = gradient_chain(
        [
            list(zip([tokens[number] for number in range(batch)], d_query)),
            list(zip(token_each, d_key_value)),
        ],
        (query_rows, d_key_value),
        extra,
    )
    query_rows, d_key_value = pumped(
        (query_rows, d_key_value), mid_chain, out_chain, token_chains[0]
    )
    query_rows = pumped(query_rows, attn_chain, in_chain)
    d_tokens = d_first_sum + right_transposed(query_rows, attn_q)
    timeline.token = d_tokens.reshape(tokens.shape)
    early, late = token_chains[0], token_chains[-1]
    ahead = [mid_chain, out_chain, attn_chain, late, in_chain, attn_chain, mid_chain]
    ahead += [attn_chain, in_chain, mid_chain, attn_chain, early, mid_chain, attn_chain]
    chains = [attn_chain, mid_chain, in_chain, out_chain, enc_chain]
    grad_attn, middle, grad_in, grad_ffn_out, d_encoded, *d_parts = finished(
        *chains, *token_chains, ahead=ahead
    )
    d_tokens, timeline.token = timeline.token, None
    d_tokens = d_tokens + (d_parts[0] if paired else jnp.stack(d_parts))
    if slotted:
        mine = grad_attn[:, 3 * width :].T
    else:
        vector_grads = jnp.zeros((vectors, width), WIDE)
        for value, first, at, count in extra:
            vector_grads = vector_grads.at[at : at + count].set(value[first : first + count])
        (vector_grads,) = finished(Chain(small_steps(vector_grads)))
        mine = lax.dynamic_slice_in_dim(vector_grads, owner * part, part, axis=1)
    grad_cross_out = grad_in[:, hidden_width:]
    return (
        final.reshape(batch, local_len, width),
        d_tokens,
        d_encoded,
        grad_attn[:, : 3 * width],
        middle[:, :width],
        middle[:, width : 4 * width],
        grad_cross_out,
        grad_in[:, :hidden_width],
        grad_ffn_out,
        mine[:gain_rows],
        mine[gain_rows : gain_rows + bias_rows],
        mine[gain_rows + bias_rows : vectors].reshape(-1),
    )


def solution(mesh):
    split = P("dp", "seq", None)
    rows = P("dp", None)
    columns = P(None, "dp")
    vector = P("dp")
    in_specs = (split,) * 3 + (rows,) * 6 + (columns, columns, vector, rows, vector)
    out_specs = (split,) * 3 + (rows,) * 6 + (columns, columns, vector)
    return jax.shard_map(local, mesh=mesh, in_specs=in_specs, out_specs=out_specs, check_vma=False)
```
